32 devices in a mesh: seq: 16 (over z, y, core), dp: 2 (over x).
Axes of the slice: x: 2, y: 2, z: 4, core: 2. Of those that a mesh axis runs over, the one named last changes fastest.
Arguments:
- queries: bfloat16 [2, 4096, 2048], P('dp', 'seq'), may hold values from -6 to 6
- key_rows: bfloat16 [2, 4096, 2048], P('dp', 'seq'), may hold values from -6 to 6
- value_rows: bfloat16 [2, 4096, 2048], P('dp', 'seq'), may hold values from -6 to 6
- out_grad: bfloat16 [2, 4096, 2048], P('dp', 'seq'), may hold values from -6 to 6
- out_weight: bfloat16 [2048, 2048], P('seq', 'dp'), may hold values from -0.125 to 0.125
Outputs:
- query_grad: bfloat16 [2, 4096, 2048], P('dp', 'seq')
- key_grad: bfloat16 [2, 4096, 2048], P('dp', 'seq')
- value_grad: bfloat16 [2, 4096, 2048], P('dp', 'seq')
- weight_grad: float32 [2048, 2048], P('seq', 'dp')
The draws below stay inside these ranges and needn't reach their ends.
All inputs are finite; a program needn't handle non-finite values.
Results may differ from the reference program's by a relative error of at most 0.014.
Values may be sent and summed in bfloat16 or wider, within the bound.
A program may use at most 192 MiB of HBM per device.

```python
import math
import jax
import jax.numpy as jnp
from jax import lax

HEADS = 16
HEAD = 128
DW = 2048
TOK_DEV = 256
HD = 2048
LENGTH = 4096
NSEQ = 2


def raised(values, own_key, source, target, blocks, factor):
    def block_of(position):
        return (jnp.arange(values.shape[position]) // (values.shape[position] // blocks)).reshape((-1,) + (1,) * (values.ndim - 1 - position))

    one_side = jax.random.permutation(own_key, blocks)[block_of(target)]
    second = (block_of(target) + blocks // 2) % blocks
    return jnp.where((block_of(source) == one_side) | (block_of(source) == second), factor * values, values)


def shard_levels(key, shape, pieces, least, largest):
    level = 1.0
    for position, parts in pieces:
        draws = jax.random.uniform(jax.random.fold_in(jax.random.fold_in(key, 6), position), (parts,), jnp.float32, least / len(pieces), largest / len(pieces))
        level = level * jnp.repeat(jnp.exp(draws), shape[position] // parts).reshape((-1,) + (1,) * (len(shape) - 1 - position))
    return level


def centred(rng, extent, scale, most, cuts=(), kind=jnp.bfloat16):
    factor_of = shard_levels(rng, extent, cuts, -0.22, 0.18) if cuts else 1.0
    entries = jax.random.normal(rng, extent, jnp.float32) * scale * factor_of
    return jnp.minimum(jnp.maximum(entries, -most), most).astype(kind)


def noise_with(rng, extent, width, bound, cuts, heavy, kind=jnp.bfloat16):
    drawn = width * jax.random.normal(rng, extent, jnp.float32)
    if cuts:
        drawn = drawn * shard_levels(rng, extent, cuts, -0.22, 0.18)
    return jnp.clip(raised(drawn, jax.random.fold_in(rng, 3), *heavy), -bound, bound).astype(kind)


def setup_inputs(seed: int = 0) -> dict:
    keys = jax.random.split(jax.random.key(seed), 6)
    return {
        "queries": centred(keys[0], (NSEQ, LENGTH, HD), 1.0, 6.0, ((0, 2), (1, 16))),
        "key_rows": centred(keys[1], (NSEQ, LENGTH, HD), 1.0, 6.0, ((0, 2), (1, 16))),
        "value_rows": centred(keys[2], (NSEQ, LENGTH, HD), 1.0, 6.0, ((0, 2), (1, 16))),
        "out_grad": noise_with(keys[3], (NSEQ, LENGTH, DW), 1.0, 6.0, ((0, 2), (1, 16)), (1, 2, 16, 2.0)),
        "out_weight": centred(keys[4], (HD, DW), HD ** -0.5, 0.125, ((0, 16), (1, 2))),
    }


def settle(values_in):
    return lax.optimization_barrier(values_in.astype(jnp.bfloat16)).astype(jnp.float32)

def reference(queries, key_rows, value_rows, out_grad, out_weight):
    seq_count = queries.shape[0]
    seq_length = queries.shape[1]
    blocks = seq_length // TOK_DEV
    score_scale = 1.0 / math.sqrt(HEAD * seq_length)
    grad_scale = 1.0 / math.sqrt(seq_count * seq_length)
    row_ids = jnp.arange(TOK_DEV, dtype=jnp.int32)
    causal = (row_ids[:, None] >= row_ids[None, :]).astype(jnp.float32)

    def split_heads(block_rows):
        return block_rows.reshape(TOK_DEV, HEADS, HEAD).astype(jnp.float32)

    def one_sequence(seq_item):
        query_seq, key_seq, value_seq, grad_seq = seq_item
        query_blocks = query_seq.reshape(blocks, TOK_DEV, HD)
        key_blocks = key_seq.reshape(blocks, TOK_DEV, HD)
        value_blocks = value_seq.reshape(blocks, TOK_DEV, HD)
        grad_blocks = grad_seq.reshape(blocks, TOK_DEV, DW)

        def forward(carry, block_item):
            kv_state, weight_acc = carry
            query_b, key_b, value_b, grad_b = block_item
            query_h = split_heads(query_b)
            key_h = split_heads(key_b)
            value_h = split_heads(value_b)
            prefix_scaled = settle(score_scale * kv_state)
            scores = settle(score_scale * jnp.einsum('thd,shd->hts', query_h, key_h) * causal)
            attended = jnp.einsum('hts,shd->thd', scores, value_h) + jnp.einsum('thd,hde->the', query_h, prefix_scaled)
            attended = attended.astype(jnp.bfloat16).reshape(TOK_DEV, HD)
            head_grad = jnp.dot(grad_b, out_weight.T, preferred_element_type=jnp.float32).astype(jnp.bfloat16)
            weight_acc = weight_acc + grad_scale * jnp.dot(attended.T, grad_b, preferred_element_type=jnp.float32)
            query_dout = jnp.einsum('thd,the->hde', query_h, split_heads(head_grad))
            kv_state = kv_state + jnp.einsum('shd,she->hde', key_h, value_h)
            return ((kv_state, weight_acc), (prefix_scaled, head_grad, query_dout))
        start_state = jnp.zeros((HEADS, HEAD, HEAD), jnp.float32)
        start_weight = jnp.zeros((HD, DW), jnp.float32)
        (_, weight_acc), (prefixes, head_grads, query_douts) = lax.scan(forward, (start_state, start_weight), (query_blocks, key_blocks, value_blocks, grad_blocks))

        def backward(grad_state, local_sum):
            return (grad_state + local_sum, grad_state)
        _, suffixes = lax.scan(backward, start_state, query_douts, reverse=True)

        def gradients(dummy, block_item):
            query_b, key_b, value_b, head_grad, prefix_scaled, suffix = block_item
            query_h = split_heads(query_b)
            key_h = split_heads(key_b)
            value_h = split_heads(value_b)
            grad_h = split_heads(head_grad)
            suffix_scaled = settle(score_scale * suffix)
            scores = settle(score_scale * jnp.einsum('thd,shd->hts', query_h, key_h) * causal)
            grad_scores = settle(score_scale * jnp.einsum('the,she->hts', grad_h, value_h) * causal)
            query_g = jnp.einsum('hts,shd->thd', grad_scores, key_h) + jnp.einsum('the,hde->thd', grad_h, prefix_scaled)
            key_g = jnp.einsum('hts,thd->shd', grad_scores, query_h) + jnp.einsum('she,hde->shd', value_h, suffix_scaled)
            value_g = jnp.einsum('hts,the->she', scores, grad_h) + jnp.einsum('shd,hde->she', key_h, suffix_scaled)
            return (dummy, (query_g.astype(jnp.bfloat16).reshape(TOK_DEV, HD), key_g.astype(jnp.bfloat16).reshape(TOK_DEV, HD), value_g.astype(jnp.bfloat16).reshape(TOK_DEV, HD)))
        _, (query_gs, key_gs, value_gs) = lax.scan(gradients, jnp.zeros((), jnp.float32), (query_blocks, key_blocks, value_blocks, head_grads, prefixes, suffixes))
        return (query_gs.reshape(seq_length, HD), key_gs.reshape(seq_length, HD), value_gs.reshape(seq_length, HD), weight_acc)
    query_grad, key_grad, value_grad, weight_parts = lax.map(one_sequence, (queries, key_rows, value_rows, out_grad))
    return (query_grad, key_grad, value_grad, lax.optimization_barrier(jnp.sum(weight_parts, axis=0)))
```

```python
import functools
import math

import jax
import jax.numpy as jnp
from jax import lax
from jax.experimental import pallas as pl
from jax.experimental.pallas import tpu as pltpu
from jax.sharding import PartitionSpec as P

HEADS = 16
HEAD = 128
HD = 2048


STREAMS = 4
MESH = pl.DeviceIdType.MESH


def log2(count):
    return count.bit_length() - 1


def stream_bits(stream, seq_count, data_count):
    high = [("seq", bit) for bit in range(log2(seq_count) - 1, 0, -1)]
    data = [("dp", bit) for bit in range(log2(data_count))]
    far, near = high[:-1], high[-1:]
    return [high + data, far + data + near, near + data + far, data + high][stream % 4]


def place(bits, seq, data):
    index = {"seq": seq, "dp": data}
    return sum((index[axis] // 2**bit) % 2 * 2**level for level, (axis, bit) in enumerate(bits))


def partner(axis, bit):
    index = lax.axis_index(axis)
    return {axis: index + (1 - 2 * ((index // 2**bit) % 2)) * 2**bit}


def greet(seq_count, data_count):
    barrier = pltpu.get_barrier_semaphore()
    bits = [("seq", 0)] + stream_bits(0, seq_count, data_count)
    for axis, bit in bits:
        pl.semaphore_signal(barrier, inc=1, device_id=partner(axis, bit), device_id_type=MESH)
    pl.semaphore_wait(barrier, len(bits))


def remote(src, dst, send, recv, device):
    return pltpu.make_async_remote_copy(
        src_ref=src, dst_ref=dst, send_sem=send, recv_sem=recv, device_id=device, device_id_type=MESH
    )


def contract(left, right, left_dim, right_dim):
    return lax.dot_general(
        left, right, (((left_dim,), (right_dim,)), ((), ())), preferred_element_type=jnp.float32
    )


def each_head(begin, end, together, body):
    whole = begin + (end - begin) // together * together

    @pl.loop(begin, whole, step=together)
    def _(h):
        for store in [body(h + i) for i in range(together)]:
            store()

    for store in [body(h) for h in range(whole, end)]:
        store()


def sum_steps(part, result, scale, reverse, scratch, seq_count):
    out16, in16, total, before, outs, ins, send_sem, recv_sem = scratch
    seq = lax.axis_index("seq")
    core = seq % 2
    half = before.shape[0]
    own = pl.ds(pl.multiple_of(core * half, half), half)
    other = pl.ds(pl.multiple_of((1 - core) * half, half), half)
    hops = log2(seq_count) - 1

    def flag(bit):
        set_bit = (seq // 2**bit) % 2
        return ((1 - set_bit) if reverse else set_bit).astype(jnp.float32)

    def pair_hop():
        return remote(out16, in16, send_sem.at[0], recv_sem.at[0], partner("seq", 0))

    def chip_hop(level):
        return remote(
            outs.at[level], ins.at[level], send_sem.at[level + 1], recv_sem.at[level + 1],
            partner("seq", level + 1) if level < hops else partner("seq", 0),
        )

    def first():
        out16[...] = part[...].astype(jnp.bfloat16)
        pair_hop().start()

    def second():
        pair_hop().wait()
        total[...] = part[own, :] + in16[own, :].astype(jnp.float32)
        before[...] = jnp.zeros_like(before)
        outs[0] = total[...].astype(jnp.bfloat16)
        chip_hop(0).start()

    def next_hop(level):
        chip_hop(level).wait()
        got = ins[level].astype(jnp.float32)
        before[...] += flag(level + 1) * got
        if level + 1 < hops:
            total[...] += got
            outs[level + 1] = total[...].astype(jnp.bfloat16)
        else:
            outs[level + 1] = before[...].astype(jnp.bfloat16)
        chip_hop(level + 1).start()

    def last():
        chip_hop(hops).wait()
        result[own, :] = (
            scale * (before[...] + flag(0) * in16[own, :].astype(jnp.float32))
        ).astype(jnp.bfloat16)
        result[other, :] = (
            scale
            * (ins[hops].astype(jnp.float32) + flag(0) * in16[other, :].astype(jnp.float32))
        ).astype(jnp.bfloat16)

    return [first, second] + [functools.partial(next_hop, level) for level in range(hops)] + [last]


def kernel(
    seq_count, data_count, score_scale, grad_scale,
    query_ref, key_ref, value_ref, grad_ref, weight_ref,
    query_out, key_out, value_out, weight_out,
    held, sums, arrived, sib_grad, head_grad, away, landed, att, sib_att,
    scores, key_sum, value_sum, part, prefix, suffix,
    out16, in16, total, before, outs, ins,
    gather_send, gather_recv, reduce_send, reduce_recv, pair_send, pair_recv,
    scan_send, scan_recv,
):
    seq, data = lax.axis_index("seq"), lax.axis_index("dp")
    core = seq % 2
    sibling = partner("seq", 0)
    rows, columns = held.shape[2], held.shape[3]
    tokens = grad_ref.shape[0]
    shard_rows = rows * STREAMS
    orders = [stream_bits(s, seq_count, data_count) for s in range(STREAMS)]
    slots = [place(orders[s], seq, data) for s in range(STREAMS)]
    levels = len(orders[0])
    group = max(1, 256 // shard_rows)
    causal = (
        lax.broadcasted_iota(jnp.int32, (tokens, tokens), 0)
        >= lax.broadcasted_iota(jnp.int32, (tokens, tokens), 1)
    ).astype(jnp.float32)

    def head_columns(h):
        return pl.ds(h * HEAD if isinstance(h, int) else pl.multiple_of(h * HEAD, HEAD), HEAD)

    for s in range(STREAMS):
        held[s, slots[s]] = weight_ref[s * rows : (s + 1) * rows, :]
    greet(seq_count, data_count)

    def gather_hop(s, level):
        size = 2**level
        block = held.at[s, pl.ds(slots[s] // size * size, size)]
        axis, bit = orders[s][level]
        return remote(
            block, block, gather_send.at[s, level], gather_recv.at[s, level], partner(axis, bit)
        )

    def gather_level(level):
        for s in range(STREAMS):
            gather_hop(s, level).wait()
            if level + 1 < levels:
                gather_hop(s, level + 1).start()

    def reduce_hop(s, level):
        size = 2**level
        mine = slots[s] // size
        theirs = mine + 1 - 2 * (mine % 2)
        axis, bit = orders[s][level]
        return remote(
            sums.at[s, pl.ds(theirs * size, size)],
            arrived.at[s, pl.ds(size, size)],
            reduce_send.at[s, level],
            reduce_recv.at[s, level],
            partner(axis, bit),
        )

    def reduce_level(level):
        size = 2**level
        for s in range(STREAMS):
            reduce_hop(s, level).wait()
            start = slots[s] // size * size
            if level == 0:
                weight_out[s * rows : (s + 1) * rows, :] = sums[s, slots[s]].astype(
                    jnp.float32
                ) + arrived[s, 1].astype(jnp.float32)
                continue

            @pl.loop(0, size)
            def _(step):
                added = sums[s, start + step].astype(jnp.float32) + arrived[
                    s, size + step
                ].astype(jnp.float32)
                sums[s, start + step] = added.astype(jnp.bfloat16)

            reduce_hop(s, level - 1).start()

    def swap(src, dst, index):
        return remote(src, dst, pair_send.at[index], pair_recv.at[index], sibling)

    for s in range(STREAMS):
        gather_hop(s, 0).start()
    grad_swap = swap(grad_ref, sib_grad, 0)
    grad_swap.start()

    def store(ref, index, value):
        ref[index] = value

    def key_value(h):
        at = head_columns(h)
        product = contract(key_ref[:, at], value_ref[:, at], 0, 0)
        return functools.partial(store, part, (at, slice(None)), product)

    each_head(0, HEADS, 4, key_value)

    scan = (out16, in16, total, before, outs, ins)
    steps = sum_steps(
        part, prefix, score_scale, False,
        tuple(ref.at[0] for ref in scan + (scan_send, scan_recv)), seq_count,
    )
    steps[0]()

    def head_scores(h):
        at = head_columns(h)
        product = score_scale * contract(query_ref[:, at], key_ref[:, at], 1, 1) * causal
        return functools.partial(store, scores, h, product.astype(jnp.bfloat16))

    each_head(0, HEADS, 4, head_scores)

    for index in range(max(len(steps) - 1, levels - 1)):
        if index + 1 < len(steps):
            steps[index + 1]()
        if index < levels - 1:
            gather_level(index)

    def head_attended(h):
        at = head_columns(h)
        attended = contract(scores[h], value_ref[:, at], 1, 0)
        attended = attended + contract(query_ref[:, at], prefix[at, :], 1, 0)
        turned = attended.T.astype(jnp.bfloat16)
        pieces = HEAD // shard_rows

        def put():
            for piece in range(pieces):
                shard = h * pieces + piece
                top = pl.multiple_of(shard // 2 * shard_rows, shard_rows)
                att[shard % 2, pl.ds(top, shard_rows), :] = turned[
                    piece * shard_rows : (piece + 1) * shard_rows, :
                ]

        return put

    each_head(0, HEADS, 4, head_attended)

    att_swap = swap(att.at[1 - core], sib_att, 1)
    att_swap.start()
    grad_swap.wait()
    att_swap.wait()
    height = group * shard_rows
    for first in range(0, seq_count // 2, group):
        strip = pl.ds(first * shard_rows, height)
        for d in range(data_count):
            across = slice(d * columns, (d + 1) * columns)
            panel = contract(att[core, strip, :], grad_ref[:, across], 1, 0)
            panel = panel + contract(sib_att[strip, :], sib_grad[:, across], 1, 0)
            panel = (grad_scale * panel).astype(jnp.bfloat16)
            for g in range(group):
                for s in range(STREAMS):
                    top = (g * STREAMS + s) * rows
                    sums[s, place(orders[s], 2 * (first + g), d)] = panel[top : top + rows, :]
    for s in range(STREAMS):
        reduce_hop(s, levels - 1).start()

    gather_level(levels - 1)
    half = away.shape[1]
    for first in range(0, seq_count // 2, group):
        panel = jnp.concatenate(
            [
                jnp.concatenate(
                    [held[s, place(orders[s], 2 * j, d)] for d in range(data_count)], axis=1
                )
                for j in range(first, first + group)
                for s in range(STREAMS)
            ],
            axis=0,
        )
        strip = slice(first * shard_rows, first * shard_rows + height)
        away[:, strip] = contract(sib_grad[...], panel, 1, 1).astype(jnp.bfloat16)
        mine = contract(grad_ref[...], panel, 1, 1).astype(jnp.bfloat16)
        for side in range(2):

            @pl.when(core == side)
            def _():
                for g in range(group):
                    left = (2 * (first + g) + side) * shard_rows
                    head_grad[:, left : left + shard_rows] = mine[
                        :, g * shard_rows : (g + 1) * shard_rows
                    ]

    back = swap(away, landed, 2)
    back.start()
    back.wait()
    for side in range(2):

        @pl.when(core != side)
        def _():
            for j in range(seq_count // 2):
                left = (2 * j + side) * shard_rows
                head_grad[:, left : left + shard_rows] = landed[
                    :, j * shard_rows : (j + 1) * shard_rows
                ]

    def query_dout(h):
        at = head_columns(h)
        product = contract(query_ref[:, at], head_grad[:, at], 0, 0)
        return functools.partial(store, part, (at, slice(None)), product)

    each_head(0, HEADS, 4, query_dout)

    steps = sum_steps(
        part, suffix, score_scale, True,
        tuple(ref.at[1] for ref in scan + (scan_send, scan_recv)), seq_count,
    )
    steps[0]()

    def local_head(h):
        at = head_columns(h)
        rows_g, rows_q, rows_k = head_grad[:, at], query_ref[:, at], key_ref[:, at]
        grad_scores = (
            score_scale * contract(rows_g, value_ref[:, at], 1, 1) * causal
        ).astype(jnp.bfloat16)
        queried = contract(grad_scores, rows_k, 1, 0) + contract(rows_g, prefix[at, :], 1, 1)
        keyed = contract(grad_scores, rows_q, 0, 0)
        valued = contract(scores[h], rows_g, 0, 0)

        def put():
            query_out[:, at] = queried.astype(jnp.bfloat16)
            key_sum[:, at] = keyed
            value_sum[:, at] = valued

        return put

    chunks = len(steps) - 1
    for index in range(max(chunks, levels - 1)):
        if index < chunks:
            each_head(HEADS * index // chunks, HEADS * (index + 1) // chunks, 4, local_head)
            steps[index + 1]()
        if index < levels - 1:
            reduce_level(levels - 1 - index)

    def last_terms(h):
        at = head_columns(h)
        keyed = key_sum[:, at] + contract(value_ref[:, at], suffix[at, :], 1, 1)
        valued = value_sum[:, at] + contract(key_ref[:, at], suffix[at, :], 1, 0)

        def put():
            key_out[:, at] = keyed.astype(jnp.bfloat16)
            value_out[:, at] = valued.astype(jnp.bfloat16)

        return put

    each_head(0, HEADS, 4, last_terms)

    reduce_level(0)


def shards(queries, key_rows, value_rows, out_grad, out_weight):
    tokens = queries.shape[1]
    seq_count = lax.axis_size("seq")
    data_count = lax.axis_size("dp")
    seq_length = tokens * seq_count
    score_scale = 1.0 / math.sqrt(HEAD * seq_length)
    grad_scale = 1.0 / math.sqrt(queries.shape[0] * data_count * seq_length)
    features = queries.shape[2]
    shard_rows, columns = out_weight.shape
    width = out_grad.shape[2]
    hops = log2(seq_count // 2)
    levels = hops + log2(data_count)
    bf16, f32 = jnp.bfloat16, jnp.float32
    blocks = (STREAMS, 2**levels, shard_rows // STREAMS, columns)
    half = features // 2
    vmem = pl.BlockSpec(memory_space=pltpu.VMEM)
    dma = pltpu.SemaphoreType.DMA
    flat = pltpu.VMEM((tokens, features), bf16)
    query_grad, key_grad, value_grad, weight_grad = pl.pallas_call(
        functools.partial(kernel, seq_count, data_count, score_scale, grad_scale),
        out_shape=(flat, flat, flat, pltpu.VMEM((shard_rows, columns), f32)),
        in_specs=[vmem] * 5,
        out_specs=(vmem,) * 4,
        scratch_shapes=[
            pltpu.VMEM(blocks, bf16),
            pltpu.VMEM(blocks, bf16),
            pltpu.VMEM(blocks, bf16),
            pltpu.VMEM((tokens, width), bf16),
            pltpu.VMEM((tokens, features), bf16),
            pltpu.VMEM((tokens, half), bf16),
            pltpu.VMEM((tokens, half), bf16),
            pltpu.VMEM((2, half, tokens), bf16),
            pltpu.VMEM((half, tokens), bf16),
            pltpu.VMEM((HEADS, tokens, tokens), bf16),
            pltpu.VMEM((tokens, features), f32),
            pltpu.VMEM((tokens, features), f32),
            pltpu.VMEM((features, HEAD), f32),
            pltpu.VMEM((features, HEAD), bf16),
            pltpu.VMEM((features, HEAD), bf16),
            pltpu.VMEM((2, features, HEAD), bf16),
            pltpu.VMEM((2, features, HEAD), bf16),
            pltpu.VMEM((2, half, HEAD), f32),
            pltpu.VMEM((2, half, HEAD), f32),
            pltpu.VMEM((2, hops + 1, half, HEAD), bf16),
            pltpu.VMEM((2, hops + 1, half, HEAD), bf16),
            dma((STREAMS, levels)),
            dma((STREAMS, levels)),
            dma((STREAMS, levels)),
            dma((STREAMS, levels)),
            dma((3,)),
            dma((3,)),
            dma((2, hops + 2)),
            dma((2, hops + 2)),
        ],
        compiler_params=pltpu.CompilerParams(
            collective_id=0, has_side_effects=True, vmem_limit_bytes=50 << 20
        ),
    )(queries[0], key_rows[0], value_rows[0], out_grad[0], out_weight)
    return query_grad[None], key_grad[None], value_grad[None], weight_grad


def solution(mesh):
    return jax.shard_map(
        shards,
        mesh=mesh,
        in_specs=(
            P("dp", "seq", None),
            P("dp", "seq", None),
            P("dp", "seq", None),
            P("dp", "seq", None),
            P("seq", "dp"),
        ),
        out_specs=(
            P("dp", "seq", None),
            P("dp", "seq", None),
            P("dp", "seq", None),
            P("seq", "dp"),
        ),
        check_vma=False,
    )
```

```python
import functools
import math

import jax
import jax.numpy as jnp
from jax import lax
from jax.experimental import pallas as pl
from jax.experimental.pallas import tpu as pltpu
from jax.sharding import PartitionSpec as P

HEADS = 16
HEAD = 128
WIDE = 256
CHUNKS = 4
MESH = pl.DeviceIdType.MESH


def remote(src, dst, send, recv, device):
    return pltpu.make_async_remote_copy(
        src_ref=src, dst_ref=dst, send_sem=send, recv_sem=recv, device_id=device, device_id_type=MESH
    )


def contract(left, right, left_dim, right_dim):
    return lax.dot_general(
        left, right, (((left_dim,), (right_dim,)), ((), ())), preferred_element_type=jnp.float32
    )


def each(begin, count, together, body):
    @pl.loop(0, count, step=together)
    def _(j):
        for store in [body(begin + j + i) for i in range(together)]:
            store()


def kernel(
    lines, data_count, score_scale, grad_scale,
    query_ref, key_ref, value_ref, grad_ref, weight_ref,
    query_out, key_out, value_out, weight_out,
    wall, others, att_own, att_in, grad_send, head_grad, scores, key_sum, value_sum,
    part, total, pair_out, pair_in, chain_in, chain_out, side_in, side_out, final_out, states,
    own_sum, x_out, x_in, z_out, z_in,
    zg_send, zg_recv, xg_send, xg_recv, o_send, o_recv, a_send, a_recv, g_send, g_recv,
    s_send, s_recv, xr_send, xr_recv, zr_send, zr_recv,
):
    f32, bf16 = jnp.float32, jnp.bfloat16
    seq, d = lax.axis_index("seq"), lax.axis_index("dp")
    k, m, y, c = seq // 4, seq % 4, (seq // 2) % 2, seq % 2
    rows, columns = weight_ref.shape
    half = rows // 2
    tokens = grad_ref.shape[0]
    span = WIDE // rows
    groups = lines // span
    per_pair = 2 * rows // HEAD
    pieces = HEAD // rows
    members = [m, m + 1 - 2 * c, m + 2 - 4 * y, 3 - m]
    peers = [{"seq": seq - m + member} for member in members]
    sib, side = peers[1], peers[2]
    above, below = {"seq": seq + 4}, {"seq": seq - 4}
    right, left = {"dp": d + 1}, {"dp": d - 1}
    causal = (
        lax.broadcasted_iota(jnp.int32, (tokens, tokens), 0)
        >= lax.broadcasted_iota(jnp.int32, (tokens, tokens), 1)
    ).astype(f32)
    pending = []

    def when(condition, body):
        if condition is True:
            body()
        elif condition is not False:
            pl.when(condition)(body)

    def start(copy, condition=True):
        when(condition, lambda: copy().start())
        pending.append((condition, copy))

    def arrive(copy, condition=True):
        when(condition, lambda: copy().wait_recv())

    barrier = pltpu.get_barrier_semaphore()
    neighbours = [(True, peer) for peer in peers[1:]]
    neighbours += [(k < lines - 1, above), (k > 0, below), (d < data_count - 1, right), (d > 0, left)]
    for condition, device in neighbours:
        when(
            condition,
            lambda device=device: pl.semaphore_signal(
                barrier, inc=1, device_id=device, device_id_type=MESH
            ),
        )
    pl.semaphore_wait(
        barrier,
        sum(1 if condition is True else jnp.where(condition, 1, 0) for condition, _ in neighbours),
    )

    def at_head(h):
        return pl.ds(pl.multiple_of(h * HEAD, HEAD), HEAD)

    def parts_of(h):
        return [h * pieces + piece for piece in range(pieces)]

    def locate(n):
        line = n // 4
        return n % 4, line // span, line % span

    def state_of(index, h):
        found = []
        for n in parts_of(h):
            member, g, j = locate(n)
            found.append(
                states[index, member % 2, member // 2, g, pl.ds(pl.multiple_of(j * rows, rows), rows), :]
            )
        return found[0] if pieces == 1 else jnp.concatenate(found, axis=0)

    def put_part(h, product):
        for piece, n in enumerate(parts_of(h)):
            member, g, j = locate(n)
            part[member % 2, member // 2, g, pl.ds(pl.multiple_of(j * rows, rows), rows), :] = product[
                piece * rows : (piece + 1) * rows, :
            ]

    def grad_of(h):
        found = []
        for n in parts_of(h):
            member, g, j = locate(n)
            if pieces == 1:
                return head_grad[member, g, :, pl.ds(pl.multiple_of(j * rows, rows), rows)]
            lane = pl.ds(pl.multiple_of(j // pieces * HEAD, HEAD), HEAD)
            block = head_grad[member, g, :, lane]
            piece = block[:, :rows]
            for i in range(1, pieces):
                piece = jnp.where(j % pieces == i, block[:, i * rows : (i + 1) * rows], piece)
            found.append(piece)
        return jnp.concatenate(found, axis=1)

    def head_of(side_bit, g, j):
        return (2 * (g * span + j // per_pair) + side_bit) * per_pair + j % per_pair

    def block_of(line, hh, column_block):
        return wall.at[column_block, pl.ds(pl.multiple_of(line * rows + hh * half, half), half)]

    def line_hop(up, hop, hh):
        line = k - hop if up else k + hop
        block = block_of(line, hh, d)
        u = int(up)
        return remote(block, block, zg_send.at[u, hop, hh], zg_recv.at[u, hop, hh], above if up else below)

    def line_send(up, hop, hh):
        valid = ((k >= hop) & (k < lines - 1)) if up else ((k + hop < lines) & (k > 0))
        start(lambda: line_hop(up, hop, hh), valid)

    def across(line, hop, hh, to_right):
        block = block_of(line, hh, d - hop if to_right else d + hop)
        u = int(to_right)
        return remote(
            block, block, xg_send.at[u, hop, hh, line], xg_recv.at[u, hop, hh, line],
            right if to_right else left,
        )

    def across_send(line, hop, hh, condition=True):
        for to_right in (True, False):
            if to_right:
                valid = (d >= hop) & (d < data_count - 1) & condition
            else:
                valid = (d + hop < data_count) & (d > 0) & condition
            start(lambda to_right=to_right: across(line, hop, hh, to_right), valid)

    def line_arrival(up, hop):
        line = k - 1 - hop if up else k + 1 + hop
        valid = (line >= 0) if up else (line < lines)
        for hh in range(2):
            block = block_of(line, hh, d)
            u = int(up)
            arrive(
                lambda: remote(block, block, zg_send.at[u, hop, hh], zg_recv.at[u, hop, hh], sib), valid
            )
            if hop + 1 < lines - 1:
                line_send(up, hop + 1, hh)
            across_send(line, 0, hh, valid)

    def across_arrivals():
        for hop in range(data_count - 1):
            for line in range(lines):
                for hh in range(2):
                    for to_right in (True, False):
                        u = int(to_right)
                        owner = d - 1 - hop if to_right else d + 1 + hop
                        valid = (owner >= 0) if to_right else (owner < data_count)
                        arrive(
                            lambda: remote(
                                block_of(line, hh, owner), block_of(line, hh, owner),
                                xg_send.at[u, hop, hh, line], xg_recv.at[u, hop, hh, line], sib,
                            ),
                            valid,
                        )
                    if hop + 1 < data_count - 1:
                        across_send(line, hop + 1, hh)

    chunk_rows = tokens // CHUNKS

    def side_rows(chunk):
        rows_at = pl.ds(chunk * chunk_rows, chunk_rows)
        return remote(
            grad_ref.at[rows_at], others.at[1, rows_at], o_send.at[0, chunk], o_recv.at[0, chunk], side
        )

    def sib_rows():
        return remote(grad_ref, others.at[0], o_send.at[2, 0], o_recv.at[2, 0], sib)

    def pass_rows(chunk):
        rows_at = pl.ds(chunk * chunk_rows, chunk_rows)
        return remote(
            others.at[1, rows_at], others.at[2, rows_at], o_send.at[1, chunk], o_recv.at[1, chunk], sib
        )

    def pass_on(chunk):
        arrive(lambda: side_rows(chunk))
        start(lambda: pass_rows(chunk))

    def grad_rows(slot):
        return grad_ref if slot == 0 else others.at[slot - 1]

    def exchange(s, kind, side_bit, g, src, dst, device):
        return remote(
            src, dst, s_send.at[s, kind, side_bit, g], s_recv.at[s, kind, side_bit, g], device
        )

    def pair_copy(s, b, g):
        return exchange(s, 0, b, g, pair_out.at[s, b, g], pair_in.at[s, b, g], sib)

    def chain_copy(s, b, g):
        return exchange(s, 1, b, g, chain_out.at[s, b, g], chain_in.at[s, b, g], below if s else above)

    def side_copy(s, b, g):
        return exchange(s, 2, b, g, side_out.at[s, b, g], side_in.at[s, b, g], side)

    def final_copy(s, b, g):
        return exchange(s, 3, b, g, final_out.at[s, b, g], states.at[s, c, b, g], sib)

    first = [k == 0, k == lines - 1]
    not_first = [k > 0, k < lines - 1]
    not_last = [k < lines - 1, k > 0]
    ahead = [(1 - y).astype(f32), y.astype(f32)]
    core = [c.astype(f32), (1 - c).astype(f32)]

    def pair_send(s, b, g):
        pair_out[s, b, g] = part[1 - c, b, g].astype(bf16)
        start(lambda: pair_copy(s, b, g))

    def pair_take(s, b, g):
        arrive(lambda: pair_copy(s, b, g))
        own = part[c, b, g]
        total[s, b, g] = own + pair_in[s, b, g].astype(f32)
        final_out[s, b, g] = own.astype(bf16)

    def chain_body(s, b, g, is_first):
        if is_first:
            chain_in[s, b, g] = jnp.zeros_like(chain_in[s, b, g])
        else:
            chain_copy(s, b, g).wait_recv()
        earlier = chain_in[s, b, g].astype(f32)
        mine = total[s, b, g]
        chain_out[s, b, g] = (earlier + mine).astype(bf16)
        when(not_last[s], lambda: chain_copy(s, b, g).start())
        side_out[s, b, g] = (earlier + ahead[s] * mine).astype(bf16)
        side_copy(s, b, g).start()

    def chain(s, chunks, step):
        here = (k == step) if s == 0 else (k == lines - 1 - step)

        def run():
            for b, g in chunks:
                chain_body(s, b, g, step == 0)

        when(here, run)

    def chain_pending(s, chunks):
        for b, g in chunks:
            pending.append((not_last[s], lambda b=b, g=g: chain_copy(s, b, g)))
            pending.append((True, lambda b=b, g=g: side_copy(s, b, g)))

    def finish(s, b, g):
        arrive(lambda: side_copy(s, b, g))
        base = chain_in[s, b, g].astype(f32) + side_in[s, b, g].astype(f32)
        mine = base + core[s] * pair_in[s, b, g].astype(f32)
        theirs = base + (1.0 - core[s]) * final_out[s, b, g].astype(f32)
        states[s, c, b, g] = (score_scale * mine).astype(bf16)
        final_out[s, b, g] = (score_scale * theirs).astype(bf16)
        start(lambda: final_copy(s, b, g))

    def final_take(s, b, g):
        arrive(
            lambda: exchange(s, 3, b, g, final_out.at[s, b, g], states.at[s, 1 - c, b, g], sib)
        )

    wall[d, pl.ds(pl.multiple_of(k * rows, rows), rows), :] = weight_ref[...]
    start(sib_rows)
    for chunk in range(CHUNKS - 1):
        start(lambda chunk=chunk: side_rows(chunk))
    for hh in range(2):
        across_send(k, 0, hh)
        line_send(False, 0, hh)

    def key_value(h):
        at = at_head(h)
        product = contract(key_ref[:, at], value_ref[:, at], 0, 0)
        return lambda: put_part(h, product)

    each(0, HEADS, 4, key_value)
    every = [(b, g) for b in range(2) for g in range(groups)]
    for b, g in every:
        pair_send(0, b, g)

    def head_scores(h):
        at = at_head(h)
        product = score_scale * contract(query_ref[:, at], key_ref[:, at], 1, 1) * causal

        def put():
            scores[h] = product.astype(bf16)

        return put

    for b, g in every:
        pair_take(0, b, g)
    chain(0, every, 0)
    for hh in range(2):
        line_send(True, 0, hh)
    each(0, HEADS, 4, head_scores)

    for hop in range(lines - 1):
        line_arrival(False, hop)
        chain(0, every, hop + 1)
        if hop == lines - 2:
            start(lambda: side_rows(CHUNKS - 1))
        line_arrival(True, hop)
        for chunk in range(CHUNKS - 1):
            if chunk * (lines - 1) // (CHUNKS - 1) == hop:
                pass_on(chunk)
    chain_pending(0, every)

    for b, g in every:
        finish(0, b, g)
    for b, g in every:
        final_take(0, b, g)

    low = k < lines // 2
    order = [jnp.where(low, groups - 1 - i, i) for i in range(groups)]

    def attend(g):
        def head_attended(h):
            at = at_head(h)
            attended = contract(scores[h], value_ref[:, at], 1, 0)
            attended = attended + contract(query_ref[:, at], state_of(0, h), 1, 0)
            turned = attended.T.astype(bf16)

            def put():
                for piece, n in enumerate(parts_of(h)):
                    member, g2, j = locate(n)
                    att_own[member, g2, pl.ds(pl.multiple_of(j * rows, rows), rows), :] = turned[
                        piece * rows : (piece + 1) * rows, :
                    ]

            return put

        each(g * (HEADS // groups), HEADS // groups, 4, head_attended)

    def att_copy(i, slot):
        g = order[i]
        return remote(
            att_own.at[members[slot], g], att_in.at[slot - 1, g],
            a_send.at[i, slot - 1], a_recv.at[i, slot - 1], peers[slot],
        )

    def head_piece(slot, g):
        rows_of = grad_rows(slot)
        product = None
        for column_block in range(data_count):
            here = pl.ds(column_block * columns, columns)
            term = contract(
                rows_of[:, here], wall[column_block, g * WIDE : (g + 1) * WIDE, :], 1, 1
            )
            product = term if product is None else product + term
        return product.astype(bf16)

    def grad_copy(slot, g):
        return remote(
            grad_send.at[slot - 1, g], head_grad.at[m, g],
            g_send.at[g, slot - 1], g_recv.at[g, slot - 1], peers[slot],
        )

    def grad_take(slot, g):
        arrive(
            lambda: remote(
                grad_send.at[slot - 1, g], head_grad.at[members[slot], g],
                g_send.at[g, slot - 1], g_recv.at[g, slot - 1], peers[slot],
            )
        )

    def send_heads(g):
        for slot in (2, 3, 1):
            grad_send[slot - 1, g] = head_piece(slot, g)
            start(functools.partial(grad_copy, slot, g))
        head_grad[m, g] = head_piece(0, g)

    for i in range(groups):
        attend(order[i])
        for slot in (2, 3, 1):
            start(functools.partial(att_copy, i, slot))
        if i == 0:
            across_arrivals()
            pass_on(CHUNKS - 1)
            arrive(sib_rows)
            for chunk in range(CHUNKS):
                arrive(lambda: pass_rows(chunk))
        send_heads(i)

    units = []
    for i in range(lines - 1):
        down = lines - 1 - i
        units.append(
            jnp.where(
                low,
                down - jnp.where(k >= down, 1, 0),
                i + jnp.where(k <= i, 1, 0),
            )
        )
    units.append(k)

    def unit_rows(t, hh):
        return pl.ds(pl.multiple_of(t * rows + hh * half, half), half)

    def weight_product(g, column_block, put):
        strip = min(columns, 512)
        for begin in range(0, columns, strip):
            here = pl.ds(pl.multiple_of(column_block * columns + begin, strip), strip)
            product = contract(att_own[m, g], grad_ref[:, here], 1, 0)
            for slot in range(1, 4):
                product = product + contract(att_in[slot - 1, g], others[slot - 1, :, here], 1, 0)
            put(slice(begin, begin + strip), grad_scale * product)

    def x_copy(u, e, t, hh):
        at = unit_rows(t, hh)
        return remote(
            x_out.at[u, e - 1, at], x_in.at[u, e - 1, at],
            xr_send.at[u, e - 1, t, hh], xr_recv.at[u, e - 1, t, hh], left if u else right,
        )

    def x_take(u, e, t, hh, condition=True):
        arrive(lambda: x_copy(u, e + 1, t, hh), condition)

    def group_rows(g):
        return pl.ds(pl.multiple_of(g * WIDE, WIDE), WIDE)

    def send_weight(i):
        g = order[i]
        for slot in (1, 2, 3):
            arrive(lambda: att_copy(i, slot))
        for e in range(data_count - 1, 0, -1):
            for u in range(2):
                valid = (d >= e) if u else (d + e < data_count)
                more = (d < data_count - 1) if u else (d > 0)
                column_block = d - e if u else d + e

                def run():
                    def put(here, value):
                        x_out[u, e - 1, group_rows(g), here] = value.astype(bf16)

                    weight_product(g, column_block, put)
                    for t in units[i * span : (i + 1) * span]:
                        for hh in range(2):
                            if e < data_count - 1:

                                @pl.when(more)
                                def _():
                                    x_copy(u, e + 1, t, hh).wait_recv()
                                    at = unit_rows(t, hh)
                                    x_out[u, e - 1, at] = (
                                        x_out[u, e - 1, at].astype(f32) + x_in[u, e, at].astype(f32)
                                    ).astype(bf16)

                            x_copy(u, e, t, hh).start()

                when(valid, run)
                for t in units[i * span : (i + 1) * span]:
                    for hh in range(2):
                        pending.append(
                            (valid, lambda u=u, e=e, t=t, hh=hh: x_copy(u, e, t, hh))
                        )

        def put_own(here, value):
            own_sum[group_rows(g), here] = value

        weight_product(g, d, put_own)

    def z_copy(u, t, hh):
        at = unit_rows(t, hh)
        return remote(
            z_out.at[at], z_in.at[u, at], zr_send.at[t, hh], zr_recv.at[u, t, hh], below if u else above
        )

    def reduce_unit(i):
        t = units[i]
        for hh in range(2):
            at = unit_rows(t, hh)

            def add(landed):
                own_sum[at, :] = own_sum[at, :] + landed[at, :].astype(f32)

            for u, condition in ((0, d > 0), (1, d < data_count - 1)):

                @pl.when(condition)
                def _():
                    x_copy(u, 1, t, hh).wait_recv()
                    add(x_in.at[u, 0])

            for u, condition in ((0, k > 0), (1, k < lines - 1)):
                moves = True if i == lines - 1 else ((t < k) if u else (t > k))

                @pl.when(condition & moves)
                def _():
                    z_copy(u, t, hh).wait_recv()
                    add(z_in.at[u])

            if i == lines - 1:
                weight_out[hh * half : (hh + 1) * half, :] = own_sum[at, :]
                continue
            z_out[at, :] = own_sum[at, :].astype(bf16)
            for u in range(2):
                start(
                    lambda u=u, t=t, hh=hh: z_copy(u, t, hh), (t < k) if u else (t > k)
                )

    def query_dout(b, g):
        def body(j):
            h = head_of(b, g, j)
            product = contract(query_ref[:, at_head(h)], grad_of(h), 0, 0)
            return lambda: put_part(h, product)

        for store in [body(j) for j in range(4)]:
            store()

    def local_heads(b, g):
        def body(j):
            h = head_of(b, g, j)
            at = at_head(h)
            rows_g, rows_q, rows_k = grad_of(h), query_ref[:, at], key_ref[:, at]
            grad_scores = (
                score_scale * contract(rows_g, value_ref[:, at], 1, 1) * causal
            ).astype(bf16)
            queried = contract(grad_scores, rows_k, 1, 0) + contract(rows_g, state_of(0, h), 1, 1)
            keyed = contract(grad_scores, rows_q, 0, 0)
            valued = contract(scores[h], rows_g, 0, 0)

            def put():
                query_out[:, at] = queried.astype(bf16)
                key_sum[:, at] = keyed
                value_sum[:, at] = valued

            return put

        for store in [body(j) for j in range(4)]:
            store()

    def last_terms(b, g):
        def body(j):
            h = head_of(b, g, j)
            at = at_head(h)
            state = state_of(1, h)
            keyed = key_sum[:, at] + contract(value_ref[:, at], state, 1, 1)
            valued = value_sum[:, at] + contract(key_ref[:, at], state, 1, 0)

            def put():
                key_out[:, at] = keyed.astype(bf16)
                value_out[:, at] = valued.astype(bf16)

            return put

        for store in [body(j) for j in range(4)]:
            store()

    near = [(y, g) for g in range(groups)]
    far = [(1 - y, g) for g in range(groups)]
    for b, g in near:
        grad_take(1, g)
        query_dout(b, g)
        pair_send(1, b, g)
    send_weight(0)
    for b, g in near:
        pair_take(1, b, g)
    chain(1, near, 0)
    for step in range(1, lines):
        if step <= groups:
            local_heads(*near[step - 1])
        chain(1, near, step)
    chain_pending(1, near)

    for i in range(groups):
        for slot in (2, 3):
            grad_take(slot, i)
        query_dout(*far[i])
        pair_send(1, *far[i])
        if i + 1 < groups:
            send_weight(i + 1)
            for j in range(span):
                reduce_unit(j)
    for b, g in far:
        pair_take(1, b, g)
    chain(1, far, 0)
    for step in range(1, lines):
        if step <= groups:
            local_heads(*far[step - 1])
        chain(1, far, step)
    chain_pending(1, far)
    for j in range(span, lines - 1):
        reduce_unit(j)
    for b, g in near + far:
        finish(1, b, g)
    reduce_unit(lines - 1)
    for b, g in near + far:
        final_take(1, b, g)
        last_terms(b, g)

    for condition, copy in pending:
        when(condition, lambda: copy().wait_send())


def shards(queries, key_rows, value_rows, out_grad, out_weight):
    tokens, features = queries.shape[1:]
    seq_count = lax.axis_size("seq")
    data_count = lax.axis_size("dp")
    lines = seq_count // 4
    seq_length = tokens * seq_count
    score_scale = 1.0 / math.sqrt(HEAD * seq_length)
    grad_scale = 1.0 / math.sqrt(queries.shape[0] * data_count * seq_length)
    rows, columns = out_weight.shape
    width = out_grad.shape[2]
    held = lines * rows
    groups = held // WIDE
    hops = max(1, data_count - 1)
    bf16, f32 = jnp.bfloat16, jnp.float32
    vmem = pl.BlockSpec(memory_space=pltpu.VMEM)
    dma = pltpu.SemaphoreType.DMA
    flat = pltpu.VMEM((tokens, features), bf16)

    def scan(kind):
        return pltpu.VMEM((2, 2, groups, WIDE, HEAD), kind)

    query_grad, key_grad, value_grad, weight_grad = pl.pallas_call(
        functools.partial(kernel, lines, data_count, score_scale, grad_scale),
        out_shape=(flat, flat, flat, pltpu.VMEM((rows, columns), f32)),
        in_specs=[vmem] * 5,
        out_specs=(vmem,) * 4,
        scratch_shapes=[
            pltpu.VMEM((data_count, held, columns), bf16),
            pltpu.VMEM((3, tokens, width), bf16),
            pltpu.VMEM((4, groups, WIDE, tokens), bf16),
            pltpu.VMEM((3, groups, WIDE, tokens), bf16),
            pltpu.VMEM((3, groups, tokens, WIDE), bf16),
            pltpu.VMEM((4, groups, tokens, WIDE), bf16),
            pltpu.VMEM((HEADS, tokens, tokens), bf16),
            pltpu.VMEM((tokens, features), f32),
            pltpu.VMEM((tokens, features), f32),
            pltpu.VMEM((2, 2, groups, WIDE, HEAD), f32),
            scan(f32),
            scan(bf16),
            scan(bf16),
            scan(bf16),
            scan(bf16),
            scan(bf16),
            scan(bf16),
            scan(bf16),
            pltpu.VMEM((2, 2, 2, groups, WIDE, HEAD), bf16),
            pltpu.VMEM((held, columns), f32),
            pltpu.VMEM((2, hops, held, columns), bf16),
            pltpu.VMEM((2, hops, held, columns), bf16),
            pltpu.VMEM((held, columns), bf16),
            pltpu.VMEM((2, held, columns), bf16),
            dma((2, lines - 1, 2)),
            dma((2, lines - 1, 2)),
            dma((2, hops, 2, lines)),
            dma((2, hops, 2, lines)),
            dma((3, CHUNKS)),
            dma((3, CHUNKS)),
            dma((groups, 3)),
            dma((groups, 3)),
            dma((groups, 3)),
            dma((groups, 3)),
            dma((2, 4, 2, groups)),
            dma((2, 4, 2, groups)),
            dma((2, hops, lines, 2)),
            dma((2, hops, lines, 2)),
            dma((lines, 2)),
            dma((2, lines, 2)),
        ],
        compiler_params=pltpu.CompilerParams(
            collective_id=0, has_side_effects=True, vmem_limit_bytes=50 << 20
        ),
    )(queries[0], key_rows[0], value_rows[0], out_grad[0], out_weight)
    return query_grad[None], key_grad[None], value_grad[None], weight_grad


def solution(mesh):
    return jax.shard_map(
        shards,
        mesh=mesh,
        in_specs=(
            P("dp", "seq", None),
            P("dp", "seq", None),
            P("dp", "seq", None),
            P("dp", "seq", None),
            P("seq", "dp"),
        ),
        out_specs=(
            P("dp", "seq", None),
            P("dp", "seq", None),
            P("dp", "seq", None),
            P("seq", "dp"),
        ),
        check_vma=False,
    )
```

```python
import functools
import math

import jax
import jax.numpy as jnp
from jax import lax
from jax.experimental import pallas as pl
from jax.experimental.pallas import tpu as pltpu
from jax.sharding import PartitionSpec as P

HEADS = 16
HEAD = 128
WIDE = 256
CHUNKS = 4
MESH = pl.DeviceIdType.MESH


def remote(src, dst, send, recv, device):
    return pltpu.make_async_remote_copy(
        src_ref=src, dst_ref=dst, send_sem=send, recv_sem=recv, device_id=device, device_id_type=MESH
    )


def contract(left, right, left_dim, right_dim):
    return lax.dot_general(
        left, right, (((left_dim,), (right_dim,)), ((), ())), preferred_element_type=jnp.float32
    )


def each(begin, count, together, body):
    @pl.loop(0, count, step=together)
    def _(j):
        for store in [body(begin + j + i) for i in range(together)]:
            store()


def kernel(
    lines, data_count, score_scale, grad_scale,
    query_ref, key_ref, value_ref, grad_ref, weight_ref,
    query_out, key_out, value_out, weight_out,
    wall, others, att_own, att_in, grad_send, head_grad, scores, key_sum, value_sum,
    part, total, pair_out, pair_in, chain_in, chain_out, side_in, side_out, final_out, states,
    own_sum, x_out, x_in, z_out, z_in,
    zg_send, zg_recv, xg_send, xg_recv, o_send, o_recv, a_send, a_recv, g_send, g_recv,
    s_send, s_recv, xr_send, xr_recv, zr_send, zr_recv,
):
    f32, bf16 = jnp.float32, jnp.bfloat16
    seq, d = lax.axis_index("seq"), lax.axis_index("dp")
    k, m, y, c = seq // 4, seq % 4, (seq // 2) % 2, seq % 2
    rows, columns = weight_ref.shape
    half = rows // 2
    tokens = grad_ref.shape[0]
    span = WIDE // rows
    groups = lines // span
    per_pair = 2 * rows // HEAD
    pieces = HEAD // rows
    members = [m, m + 1 - 2 * c, m + 2 - 4 * y, 3 - m]
    peers = [{"seq": seq - m + member} for member in members]
    sib, side = peers[1], peers[2]
    above, below = {"seq": seq + 4}, {"seq": seq - 4}
    right, left = {"dp": d + 1}, {"dp": d - 1}
    causal = (
        lax.broadcasted_iota(jnp.int32, (tokens, tokens), 0)
        >= lax.broadcasted_iota(jnp.int32, (tokens, tokens), 1)
    ).astype(f32)
    pending = []

    def when(condition, body):
        if condition is True:
            body()
        elif condition is not False:
            pl.when(condition)(body)

    def start(copy, condition=True):
        when(condition, lambda: copy().start())
        pending.append((condition, copy))

    def arrive(copy, condition=True):
        when(condition, lambda: copy().wait_recv())

    barrier = pltpu.get_barrier_semaphore()
    neighbours = [(True, peer) for peer in peers[1:]]
    neighbours += [(k < lines - 1, above), (k > 0, below), (d < data_count - 1, right), (d > 0, left)]
    for condition, device in neighbours:
        when(
            condition,
            lambda device=device: pl.semaphore_signal(
                barrier, inc=1, device_id=device, device_id_type=MESH
            ),
        )
    pl.semaphore_wait(
        barrier,
        sum(1 if condition is True else jnp.where(condition, 1, 0) for condition, _ in neighbours),
    )

    def at_head(h):
        return pl.ds(pl.multiple_of(h * HEAD, HEAD), HEAD)

    def parts_of(h):
        return [h * pieces + piece for piece in range(pieces)]

    def locate(n):
        line = n // 4
        return n % 4, line // span, line % span

    def state_of(index, h):
        found = []
        for n in parts_of(h):
            member, g, j = locate(n)
            found.append(
                states[index, member % 2, member // 2, g, pl.ds(pl.multiple_of(j * rows, rows), rows), :]
            )
        return found[0] if pieces == 1 else jnp.concatenate(found, axis=0)

    def put_part(h, product):
        for piece, n in enumerate(parts_of(h)):
            member, g, j = locate(n)
            part[member % 2, member // 2, g, pl.ds(pl.multiple_of(j * rows, rows), rows), :] = product[
                piece * rows : (piece + 1) * rows, :
            ]

    def grad_of(h):
        found = []
        for n in parts_of(h):
            member, g, j = locate(n)
            if pieces == 1:
                return head_grad[member, g, :, pl.ds(pl.multiple_of(j * rows, rows), rows)]
            lane = pl.ds(pl.multiple_of(j // pieces * HEAD, HEAD), HEAD)
            block = head_grad[member, g, :, lane]
            piece = block[:, :rows]
            for i in range(1, pieces):
                piece = jnp.where(j % pieces == i, block[:, i * rows : (i + 1) * rows], piece)
            found.append(piece)
        return jnp.concatenate(found, axis=1)

    def head_of(side_bit, g, j):
        return (2 * (g * span + j // per_pair) + side_bit) * per_pair + j % per_pair

    def block_of(line, hh, column_block):
        return wall.at[column_block, pl.ds(pl.multiple_of(line * rows + hh * half, half), half)]

    def line_hop(up, hop, hh):
        line = k - hop if up else k + hop
        block = block_of(line, hh, d)
        u = int(up)
        return remote(block, block, zg_send.at[u, hop, hh], zg_recv.at[u, hop, hh], above if up else below)

    def line_send(up, hop, hh):
        valid = ((k >= hop) & (k < lines - 1)) if up else ((k + hop < lines) & (k > 0))
        start(lambda: line_hop(up, hop, hh), valid)

    def across(line, hop, hh, to_right):
        block = block_of(line, hh, d - hop if to_right else d + hop)
        u = int(to_right)
        return remote(
            block, block, xg_send.at[u, hop, hh, line], xg_recv.at[u, hop, hh, line],
            right if to_right else left,
        )

    def across_send(line, hop, hh, condition=True):
        for to_right in (True, False):
            if to_right:
                valid = (d >= hop) & (d < data_count - 1) & condition
            else:
                valid = (d + hop < data_count) & (d > 0) & condition
            start(lambda to_right=to_right: across(line, hop, hh, to_right), valid)

    def line_arrival(up, hop):
        line = k - 1 - hop if up else k + 1 + hop
        valid = (line >= 0) if up else (line < lines)
        for hh in range(2):
            block = block_of(line, hh, d)
            u = int(up)
            arrive(
                lambda: remote(block, block, zg_send.at[u, hop, hh], zg_recv.at[u, hop, hh], sib), valid
            )
            if hop + 1 < lines - 1:
                line_send(up, hop + 1, hh)
            across_send(line, 0, hh, valid)

    def across_arrivals():
        for hop in range(data_count - 1):
            for line in range(lines):
                for hh in range(2):
                    for to_right in (True, False):
                        u = int(to_right)
                        owner = d - 1 - hop if to_right else d + 1 + hop
                        valid = (owner >= 0) if to_right else (owner < data_count)
                        arrive(
                            lambda: remote(
                                block_of(line, hh, owner), block_of(line, hh, owner),
                                xg_send.at[u, hop, hh, line], xg_recv.at[u, hop, hh, line], sib,
                            ),
                            valid,
                        )
                    if hop + 1 < data_count - 1:
                        across_send(line, hop + 1, hh)

    chunk_rows = tokens // CHUNKS

    def side_rows(chunk):
        rows_at = pl.ds(chunk * chunk_rows, chunk_rows)
        return remote(
            grad_ref.at[rows_at], others.at[1, rows_at], o_send.at[0, chunk], o_recv.at[0, chunk], side
        )

    def sib_rows():
        return remote(grad_ref, others.at[0], o_send.at[2, 0], o_recv.at[2, 0], sib)

    def pass_rows(chunk):
        rows_at = pl.ds(chunk * chunk_rows, chunk_rows)
        return remote(
            others.at[1, rows_at], others.at[2, rows_at], o_send.at[1, chunk], o_recv.at[1, chunk], sib
        )

    def pass_on(chunk):
        arrive(lambda: side_rows(chunk))
        start(lambda: pass_rows(chunk))

    def grad_rows(slot):
        return grad_ref if slot == 0 else others.at[slot - 1]

    def exchange(s, kind, side_bit, g, src, dst, device):
        return remote(
            src, dst, s_send.at[s, kind, side_bit, g], s_recv.at[s, kind, side_bit, g], device
        )

    def pair_copy(s, b, g):
        return exchange(s, 0, b, g, pair_out.at[s, b, g], pair_in.at[s, b, g], sib)

    def chain_copy(s, b, g):
        return exchange(s, 1, b, g, chain_out.at[s, b, g], chain_in.at[s, b, g], below if s else above)

    def side_copy(s, b, g):
        return exchange(s, 2, b, g, side_out.at[s, b, g], side_in.at[s, b, g], side)

    def final_copy(s, b, g):
        return exchange(s, 3, b, g, final_out.at[s, b, g], states.at[s, c, b, g], sib)

    first = [k == 0, k == lines - 1]
    not_first = [k > 0, k < lines - 1]
    not_last = [k < lines - 1, k > 0]
    ahead = [(1 - y).astype(f32), y.astype(f32)]
    core = [c.astype(f32), (1 - c).astype(f32)]

    def pair_send(s, b, g):
        pair_out[s, b, g] = part[1 - c, b, g].astype(bf16)
        start(lambda: pair_copy(s, b, g))

    def pair_take(s, b, g):
        arrive(lambda: pair_copy(s, b, g))
        own = part[c, b, g]
        total[s, b, g] = own + pair_in[s, b, g].astype(f32)
        final_out[s, b, g] = own.astype(bf16)

    def chain_body(s, b, g, is_first):
        if is_first:
            chain_in[s, b, g] = jnp.zeros_like(chain_in[s, b, g])
        else:
            chain_copy(s, b, g).wait_recv()
        earlier = chain_in[s, b, g].astype(f32)
        mine = total[s, b, g]
        chain_out[s, b, g] = (earlier + mine).astype(bf16)
        when(not_last[s], lambda: chain_copy(s, b, g).start())
        side_out[s, b, g] = (earlier + ahead[s] * mine).astype(bf16)
        side_copy(s, b, g).start()

    def chain(s, chunks, step):
        here = (k == step) if s == 0 else (k == lines - 1 - step)

        def run():
            for b, g in chunks:
                chain_body(s, b, g, step == 0)

        when(here, run)

    def chain_pending(s, chunks):
        for b, g in chunks:
            pending.append((not_last[s], lambda b=b, g=g: chain_copy(s, b, g)))
            pending.append((True, lambda b=b, g=g: side_copy(s, b, g)))

    def finish(s, b, g):
        arrive(lambda: side_copy(s, b, g))
        base = chain_in[s, b, g].astype(f32) + side_in[s, b, g].astype(f32)
        mine = base + core[s] * pair_in[s, b, g].astype(f32)
        theirs = base + (1.0 - core[s]) * final_out[s, b, g].astype(f32)
        states[s, c, b, g] = (score_scale * mine).astype(bf16)
        final_out[s, b, g] = (score_scale * theirs).astype(bf16)
        start(lambda: final_copy(s, b, g))

    def final_take(s, b, g):
        arrive(
            lambda: exchange(s, 3, b, g, final_out.at[s, b, g], states.at[s, 1 - c, b, g], sib)
        )

    wall[d, pl.ds(pl.multiple_of(k * rows, rows), rows), :] = weight_ref[...]
    start(sib_rows)
    for chunk in range(CHUNKS - 1):
        start(lambda chunk=chunk: side_rows(chunk))
    for hh in range(2):
        across_send(k, 0, hh)
        line_send(False, 0, hh)

    def key_value(h):
        at = at_head(h)
        product = contract(key_ref[:, at], value_ref[:, at], 0, 0)
        return lambda: put_part(h, product)

    each(0, HEADS, 4, key_value)
    every = [(b, g) for b in range(2) for g in range(groups)]
    for b, g in every:
        pair_send(0, b, g)

    def head_scores(h):
        at = at_head(h)
        product = score_scale * contract(query_ref[:, at], key_ref[:, at], 1, 1) * causal

        def put():
            scores[h] = product.astype(bf16)

        return put

    for b, g in every:
        pair_take(0, b, g)
    chain(0, every, 0)
    for hh in range(2):
        line_send(True, 0, hh)
    each(0, HEADS, 4, head_scores)

    for hop in range(lines - 1):
        line_arrival(False, hop)
        chain(0, every, hop + 1)
        if hop == lines - 2:
            start(lambda: side_rows(CHUNKS - 1))
        line_arrival(True, hop)
        for chunk in range(CHUNKS - 1):
            if chunk * (lines - 1) // (CHUNKS - 1) == hop:
                pass_on(chunk)
    chain_pending(0, every)

    for b, g in every:
        finish(0, b, g)
    for b, g in every:
        final_take(0, b, g)

    order = [jnp.where(k == 0, groups - 1 - i, i) for i in range(groups)]

    def attend(g):
        def head_attended(h):
            at = at_head(h)
            attended = contract(scores[h], value_ref[:, at], 1, 0)
            attended = attended + contract(query_ref[:, at], state_of(0, h), 1, 0)
            turned = attended.T.astype(bf16)

            def put():
                for piece, n in enumerate(parts_of(h)):
                    member, g2, j = locate(n)
                    att_own[member, g2, pl.ds(pl.multiple_of(j * rows, rows), rows), :] = turned[
                        piece * rows : (piece + 1) * rows, :
                    ]

            return put

        each(g * (HEADS // groups), HEADS // groups, 4, head_attended)

    def att_copy(i, slot):
        g = order[i]
        return remote(
            att_own.at[members[slot], g], att_in.at[slot - 1, g],
            a_send.at[i, slot - 1], a_recv.at[i, slot - 1], peers[slot],
        )

    def head_piece(slot, g):
        rows_of = grad_rows(slot)
        product = None
        for column_block in range(data_count):
            here = pl.ds(column_block * columns, columns)
            term = contract(
                rows_of[:, here], wall[column_block, g * WIDE : (g + 1) * WIDE, :], 1, 1
            )
            product = term if product is None else product + term
        return product.astype(bf16)

    def grad_copy(slot, g):
        return remote(
            grad_send.at[slot - 1, g], head_grad.at[m, g],
            g_send.at[g, slot - 1], g_recv.at[g, slot - 1], peers[slot],
        )

    def grad_take(slot, g):
        arrive(
            lambda: remote(
                grad_send.at[slot - 1, g], head_grad.at[members[slot], g],
                g_send.at[g, slot - 1], g_recv.at[g, slot - 1], peers[slot],
            )
        )

    def send_heads(g):
        for slot in (2, 3, 1):
            grad_send[slot - 1, g] = head_piece(slot, g)
            start(functools.partial(grad_copy, slot, g))
        head_grad[m, g] = head_piece(0, g)

    for i in range(groups):
        attend(order[i])
        for slot in (2, 3, 1):
            start(functools.partial(att_copy, i, slot))
        if i == 0:
            across_arrivals()
            pass_on(CHUNKS - 1)
            arrive(sib_rows)
            for chunk in range(CHUNKS):
                arrive(lambda: pass_rows(chunk))
        send_heads(i)

    crossing = []
    for i in range(groups):
        base = order[i] * span
        for j in range(span):
            falls = (k == 0) if i == 0 else (k < lines - 1)
            crossing.append(base + jnp.where(falls, span - 1 - j, j))
    units = [jnp.where(i < k, i, lines - 1 - i + k) for i in range(lines - 1)] + [k]

    def unit_rows(t, hh):
        return pl.ds(pl.multiple_of(t * rows + hh * half, half), half)

    def weight_product(g, column_block, put):
        strip = min(columns, 512)
        for begin in range(0, columns, strip):
            here = pl.ds(pl.multiple_of(column_block * columns + begin, strip), strip)
            product = contract(att_own[m, g], grad_ref[:, here], 1, 0)
            for slot in range(1, 4):
                product = product + contract(att_in[slot - 1, g], others[slot - 1, :, here], 1, 0)
            put(slice(begin, begin + strip), grad_scale * product)

    def x_copy(u, e, t, hh):
        at = unit_rows(t, hh)
        return remote(
            x_out.at[u, e - 1, at], x_in.at[u, e - 1, at],
            xr_send.at[u, e - 1, t, hh], xr_recv.at[u, e - 1, t, hh], left if u else right,
        )

    def x_take(u, e, t, hh, condition=True):
        arrive(lambda: x_copy(u, e + 1, t, hh), condition)

    def group_rows(g):
        return pl.ds(pl.multiple_of(g * WIDE, WIDE), WIDE)

    def send_weight(i):
        g = order[i]
        for slot in (1, 2, 3):
            arrive(lambda: att_copy(i, slot))
        for e in range(data_count - 1, 0, -1):
            for u in range(2):
                valid = (d >= e) if u else (d + e < data_count)
                more = (d < data_count - 1) if u else (d > 0)
                column_block = d - e if u else d + e

                def run():
                    def put(here, value):
                        x_out[u, e - 1, group_rows(g), here] = value.astype(bf16)

                    weight_product(g, column_block, put)
                    for t in crossing[i * span : (i + 1) * span]:
                        for hh in range(2):
                            if e < data_count - 1:

                                @pl.when(more)
                                def _():
                                    x_copy(u, e + 1, t, hh).wait_recv()
                                    at = unit_rows(t, hh)
                                    x_out[u, e - 1, at] = (
                                        x_out[u, e - 1, at].astype(f32) + x_in[u, e, at].astype(f32)
                                    ).astype(bf16)

                            x_copy(u, e, t, hh).start()

                when(valid, run)
                for t in crossing[i * span : (i + 1) * span]:
                    for hh in range(2):
                        pending.append(
                            (valid, lambda u=u, e=e, t=t, hh=hh: x_copy(u, e, t, hh))
                        )

        def put_own(here, value):
            own_sum[group_rows(g), here] = value

        weight_product(g, d, put_own)

    def z_copy(u, t, hh):
        at = unit_rows(t, hh)
        return remote(
            z_out.at[at], z_in.at[u, at], zr_send.at[t, hh], zr_recv.at[u, t, hh], below if u else above
        )

    def reduce_unit(i, here=True):
        t = units[i]

        def run():
            for hh in range(2):
                at = unit_rows(t, hh)

                def add(landed):
                    own_sum[at, :] = own_sum[at, :] + landed[at, :].astype(f32)

                for u, condition in ((0, d > 0), (1, d < data_count - 1)):

                    @pl.when(condition)
                    def _():
                        x_copy(u, 1, t, hh).wait_recv()
                        add(x_in.at[u, 0])

                for u, condition in ((0, k > 0), (1, k < lines - 1)):
                    moves = True if i == lines - 1 else ((t < k) if u else (t > k))

                    @pl.when(condition & moves)
                    def _():
                        z_copy(u, t, hh).wait_recv()
                        add(z_in.at[u])

                if i == lines - 1:
                    weight_out[hh * half : (hh + 1) * half, :] = own_sum[at, :]
                    continue
                z_out[at, :] = own_sum[at, :].astype(bf16)
                for u in range(2):
                    when((t < k) if u else (t > k), lambda: z_copy(u, t, hh).start())

        when(here, run)

    def reduce_pending(i):
        t = units[i]
        for hh in range(2):
            for u in range(2):
                pending.append(
                    ((t < k) if u else (t > k), lambda u=u, t=t, hh=hh: z_copy(u, t, hh))
                )

    def query_dout(b, g):
        def body(j):
            h = head_of(b, g, j)
            product = contract(query_ref[:, at_head(h)], grad_of(h), 0, 0)
            return lambda: put_part(h, product)

        for store in [body(j) for j in range(4)]:
            store()

    def local_heads(b, g):
        def body(j):
            h = head_of(b, g, j)
            at = at_head(h)
            rows_g, rows_q, rows_k = grad_of(h), query_ref[:, at], key_ref[:, at]
            grad_scores = (
                score_scale * contract(rows_g, value_ref[:, at], 1, 1) * causal
            ).astype(bf16)
            queried = contract(grad_scores, rows_k, 1, 0) + contract(rows_g, state_of(0, h), 1, 1)
            keyed = contract(grad_scores, rows_q, 0, 0)
            valued = contract(scores[h], rows_g, 0, 0)

            def put():
                query_out[:, at] = queried.astype(bf16)
                key_sum[:, at] = keyed
                value_sum[:, at] = valued

            return put

        for store in [body(j) for j in range(4)]:
            store()

    def last_terms(b, g):
        def body(j):
            h = head_of(b, g, j)
            at = at_head(h)
            state = state_of(1, h)
            keyed = key_sum[:, at] + contract(value_ref[:, at], state, 1, 1)
            valued = value_sum[:, at] + contract(key_ref[:, at], state, 1, 0)

            def put():
                key_out[:, at] = keyed.astype(bf16)
                value_out[:, at] = valued.astype(bf16)

            return put

        for store in [body(j) for j in range(4)]:
            store()

    near = [(y, g) for g in range(groups)]
    far = [(1 - y, g) for g in range(groups)]
    lower = (k > 0) & (k < lines // 2)
    upper = (k >= lines // 2) & (k < lines - 1)

    def reduce_units(first_set, here):
        for i in range(1, span) if first_set else range(span, lines - 1):
            reduce_unit(i, here)

    def take_far(g):
        for slot in (2, 3):
            grad_take(slot, g)
        query_dout(*far[g])
        pair_send(1, *far[g])
        pair_take(1, *far[g])
        chain(1, [far[g]], 0)

    for b, g in near:
        grad_take(1, g)
        query_dout(b, g)
        pair_send(1, b, g)
    for b, g in near:
        pair_take(1, b, g)
    chain(1, near, 0)
    send_weight(0)
    for step in range(1, lines):
        if step <= groups:
            local_heads(*near[step - 1])
        chain(1, near, step)
    take_far(0)
    local_heads(*far[0])
    chain(1, [far[0]], 1)
    send_weight(1)
    for step in range(2, lines):
        chain(1, [far[0]], step)
    reduce_unit(0)
    reduce_units(True, k == 0)
    take_far(1)
    reduce_units(True, k == lines - 1)
    local_heads(*far[1])
    chain(1, [far[1]], 1)
    reduce_units(True, lower)
    reduce_units(False, (k == 0) | (k == lines - 1))
    chain(1, [far[1]], 2)
    reduce_units(True, upper)
    for b in range(2):
        finish(1, b, 0)
    for b in range(2):
        final_take(1, b, 0)
        last_terms(b, 0)
    for step in range(3, lines):
        chain(1, [far[1]], step)
    reduce_units(False, lower | upper)
    for b in range(2):
        finish(1, b, 1)
    reduce_unit(lines - 1)
    for b in range(2):
        final_take(1, b, 1)
        last_terms(b, 1)
    chain_pending(1, near + far)
    for i in range(lines - 1):
        reduce_pending(i)

    for condition, copy in pending:
        when(condition, lambda: copy().wait_send())


def shards(queries, key_rows, value_rows, out_grad, out_weight):
    tokens, features = queries.shape[1:]
    seq_count = lax.axis_size("seq")
    data_count = lax.axis_size("dp")
    lines = seq_count // 4
    seq_length = tokens * seq_count
    score_scale = 1.0 / math.sqrt(HEAD * seq_length)
    grad_scale = 1.0 / math.sqrt(queries.shape[0] * data_count * seq_length)
    rows, columns = out_weight.shape
    width = out_grad.shape[2]
    held = lines * rows
    groups = held // WIDE
    hops = max(1, data_count - 1)
    bf16, f32 = jnp.bfloat16, jnp.float32
    vmem = pl.BlockSpec(memory_space=pltpu.VMEM)
    dma = pltpu.SemaphoreType.DMA
    flat = pltpu.VMEM((tokens, features), bf16)

    def scan(kind):
        return pltpu.VMEM((2, 2, groups, WIDE, HEAD), kind)

    query_grad, key_grad, value_grad, weight_grad = pl.pallas_call(
        functools.partial(kernel, lines, data_count, score_scale, grad_scale),
        out_shape=(flat, flat, flat, pltpu.VMEM((rows, columns), f32)),
        in_specs=[vmem] * 5,
        out_specs=(vmem,) * 4,
        scratch_shapes=[
            pltpu.VMEM((data_count, held, columns), bf16),
            pltpu.VMEM((3, tokens, width), bf16),
            pltpu.VMEM((4, groups, WIDE, tokens), bf16),
            pltpu.VMEM((3, groups, WIDE, tokens), bf16),
            pltpu.VMEM((3, groups, tokens, WIDE), bf16),
            pltpu.VMEM((4, groups, tokens, WIDE), bf16),
            pltpu.VMEM((HEADS, tokens, tokens), bf16),
            pltpu.VMEM((tokens, features), f32),
            pltpu.VMEM((tokens, features), f32),
            pltpu.VMEM((2, 2, groups, WIDE, HEAD), f32),
            scan(f32),
            scan(bf16),
            scan(bf16),
            scan(bf16),
            scan(bf16),
            scan(bf16),
            scan(bf16),
            scan(bf16),
            pltpu.VMEM((2, 2, 2, groups, WIDE, HEAD), bf16),
            pltpu.VMEM((held, columns), f32),
            pltpu.VMEM((2, hops, held, columns), bf16),
            pltpu.VMEM((2, hops, held, columns), bf16),
            pltpu.VMEM((held, columns), bf16),
            pltpu.VMEM((2, held, columns), bf16),
            dma((2, lines - 1, 2)),
            dma((2, lines - 1, 2)),
            dma((2, hops, 2, lines)),
            dma((2, hops, 2, lines)),
            dma((3, CHUNKS)),
            dma((3, CHUNKS)),
            dma((groups, 3)),
            dma((groups, 3)),
            dma((groups, 3)),
            dma((groups, 3)),
            dma((2, 4, 2, groups)),
            dma((2, 4, 2, groups)),
            dma((2, hops, lines, 2)),
            dma((2, hops, lines, 2)),
            dma((lines, 2)),
            dma((2, lines, 2)),
        ],
        compiler_params=pltpu.CompilerParams(
            collective_id=0, has_side_effects=True, vmem_limit_bytes=50 << 20
        ),
    )(queries[0], key_rows[0], value_rows[0], out_grad[0], out_weight)
    return query_grad[None], key_grad[None], value_grad[None], weight_grad


def solution(mesh):
    return jax.shard_map(
        shards,
        mesh=mesh,
        in_specs=(
            P("dp", "seq", None),
            P("dp", "seq", None),
            P("dp", "seq", None),
            P("dp", "seq", None),
            P("seq", "dp"),
        ),
        out_specs=(
            P("dp", "seq", None),
            P("dp", "seq", None),
            P("dp", "seq", None),
            P("seq", "dp"),
        ),
        check_vma=False,
    )
```

```python
import functools
import math

import jax
import jax.numpy as jnp
from jax import lax
from jax.experimental import pallas as pl
from jax.experimental.pallas import tpu as pltpu
from jax.sharding import PartitionSpec as P

HEADS = 16
HEAD = 128
WIDE = 256
CHUNKS = 4
MESH = pl.DeviceIdType.MESH


def remote(src, dst, send, recv, device):
    return pltpu.make_async_remote_copy(
        src_ref=src, dst_ref=dst, send_sem=send, recv_sem=recv, device_id=device, device_id_type=MESH
    )


def contract(left, right, left_dim, right_dim):
    return lax.dot_general(
        left, right, (((left_dim,), (right_dim,)), ((), ())), preferred_element_type=jnp.float32
    )


def each(begin, count, together, body):
    @pl.loop(0, count, step=together)
    def _(j):
        for store in [body(begin + j + i) for i in range(together)]:
            store()


def kernel(
    lines, data_count, score_scale, grad_scale,
    query_hbm, key_hbm, value_hbm, grad_hbm, weight_hbm,
    query_out, key_out, value_out, weight_out,
    query_ref, key_ref, value_ref, grad_ref, wall, others, att_own, att_in, grad_send, head_grad, scores, key_sum, value_sum,
    part, total, pair_out, pair_in, chain_in, chain_out, side_in, side_out, final_out, states,
    own_sum, x_out, x_in, z_out, z_in,
    zg_send, zg_recv, xg_send, xg_recv, o_send, o_recv, a_send, a_recv, g_send, g_recv,
    s_send, s_recv, xr_send, xr_recv, zr_send, zr_recv, load_sem,
):
    f32, bf16 = jnp.float32, jnp.bfloat16
    seq, d = lax.axis_index("seq"), lax.axis_index("dp")
    k, m, y, c = seq // 4, seq % 4, (seq // 2) % 2, seq % 2
    rows, columns = weight_hbm.shape
    half = rows // 2
    tokens = grad_ref.shape[0]
    span = WIDE // rows
    groups = lines // span
    per_pair = 2 * rows // HEAD
    pieces = HEAD // rows
    members = [m, m + 1 - 2 * c, m + 2 - 4 * y, 3 - m]
    peers = [{"seq": seq - m + member} for member in members]
    sib, side = peers[1], peers[2]
    above, below = {"seq": seq + 4}, {"seq": seq - 4}
    right, left = {"dp": d + 1}, {"dp": d - 1}
    causal = (
        lax.broadcasted_iota(jnp.int32, (tokens, tokens), 0)
        >= lax.broadcasted_iota(jnp.int32, (tokens, tokens), 1)
    ).astype(f32)
    pending = []

    def when(condition, body):
        if condition is True:
            body()
        elif condition is not False:
            pl.when(condition)(body)

    def start(copy, condition=True):
        when(condition, lambda: copy().start())
        pending.append((condition, copy))

    def arrive(copy, condition=True):
        when(condition, lambda: copy().wait_recv())

    own_rows = wall.at[d, pl.ds(pl.multiple_of(k * rows, rows), rows)]
    loads = [
        pltpu.make_async_copy(src, dst, load_sem.at[i])
        for i, (src, dst) in enumerate(
            (
                (key_hbm, key_ref), (value_hbm, value_ref), (weight_hbm, own_rows),
                (query_hbm, query_ref), (grad_hbm, grad_ref),
            )
        )
    ]
    for load in loads:
        load.start()
    barrier = pltpu.get_barrier_semaphore()
    neighbours = [(True, peer) for peer in peers[1:]]
    neighbours += [(k < lines - 1, above), (k > 0, below), (d < data_count - 1, right), (d > 0, left)]
    for condition, device in neighbours:
        when(
            condition,
            lambda device=device: pl.semaphore_signal(
                barrier, inc=1, device_id=device, device_id_type=MESH
            ),
        )
    pl.semaphore_wait(
        barrier,
        sum(1 if condition is True else jnp.where(condition, 1, 0) for condition, _ in neighbours),
    )

    def at_head(h):
        return pl.ds(pl.multiple_of(h * HEAD, HEAD), HEAD)

    def parts_of(h):
        return [h * pieces + piece for piece in range(pieces)]

    def locate(n):
        line = n // 4
        return n % 4, line // span, line % span

    def state_of(index, h):
        found = []
        for n in parts_of(h):
            member, g, j = locate(n)
            found.append(
                states[index, member % 2, member // 2, g, pl.ds(pl.multiple_of(j * rows, rows), rows), :]
            )
        return found[0] if pieces == 1 else jnp.concatenate(found, axis=0)

    def put_part(h, product):
        for piece, n in enumerate(parts_of(h)):
            member, g, j = locate(n)
            part[member % 2, member // 2, g, pl.ds(pl.multiple_of(j * rows, rows), rows), :] = product[
                piece * rows : (piece + 1) * rows, :
            ]

    def grad_of(h):
        found = []
        for n in parts_of(h):
            member, g, j = locate(n)
            if pieces == 1:
                return head_grad[member, g, :, pl.ds(pl.multiple_of(j * rows, rows), rows)]
            lane = pl.ds(pl.multiple_of(j // pieces * HEAD, HEAD), HEAD)
            block = head_grad[member, g, :, lane]
            piece = block[:, :rows]
            for i in range(1, pieces):
                piece = jnp.where(j % pieces == i, block[:, i * rows : (i + 1) * rows], piece)
            found.append(piece)
        return jnp.concatenate(found, axis=1)

    def head_of(side_bit, g, j):
        return (2 * (g * span + j // per_pair) + side_bit) * per_pair + j % per_pair

    def block_of(line, hh, column_block):
        return wall.at[column_block, pl.ds(pl.multiple_of(line * rows + hh * half, half), half)]

    def line_hop(up, hop, hh):
        line = k - hop if up else k + hop
        block = block_of(line, hh, d)
        u = int(up)
        return remote(block, block, zg_send.at[u, hop, hh], zg_recv.at[u, hop, hh], above if up else below)

    def line_send(up, hop, hh):
        valid = ((k >= hop) & (k < lines - 1)) if up else ((k + hop < lines) & (k > 0))
        start(lambda: line_hop(up, hop, hh), valid)

    def across(line, hop, hh, to_right):
        block = block_of(line, hh, d - hop if to_right else d + hop)
        u = int(to_right)
        return remote(
            block, block, xg_send.at[u, hop, hh, line], xg_recv.at[u, hop, hh, line],
            right if to_right else left,
        )

    def across_send(line, hop, hh, condition=True):
        for to_right in (True, False):
            if to_right:
                valid = (d >= hop) & (d < data_count - 1) & condition
            else:
                valid = (d + hop < data_count) & (d > 0) & condition
            start(lambda to_right=to_right: across(line, hop, hh, to_right), valid)

    def line_arrival(up, hop):
        line = k - 1 - hop if up else k + 1 + hop
        valid = (line >= 0) if up else (line < lines)
        for hh in range(2):
            block = block_of(line, hh, d)
            u = int(up)
            arrive(
                lambda: remote(block, block, zg_send.at[u, hop, hh], zg_recv.at[u, hop, hh], sib), valid
            )
            if hop + 1 < lines - 1:
                line_send(up, hop + 1, hh)
            across_send(line, 0, hh, valid)

    def across_arrivals():
        for hop in range(data_count - 1):
            for line in range(lines):
                for hh in range(2):
                    for to_right in (True, False):
                        u = int(to_right)
                        owner = d - 1 - hop if to_right else d + 1 + hop
                        valid = (owner >= 0) if to_right else (owner < data_count)
                        arrive(
                            lambda: remote(
                                block_of(line, hh, owner), block_of(line, hh, owner),
                                xg_send.at[u, hop, hh, line], xg_recv.at[u, hop, hh, line], sib,
                            ),
                            valid,
                        )
                    if hop + 1 < data_count - 1:
                        across_send(line, hop + 1, hh)

    chunk_rows = tokens // CHUNKS

    def side_rows(chunk):
        rows_at = pl.ds(chunk * chunk_rows, chunk_rows)
        return remote(
            grad_hbm.at[rows_at], others.at[1, rows_at], o_send.at[0, chunk], o_recv.at[0, chunk], side
        )

    def sib_rows():
        return remote(grad_hbm, others.at[0], o_send.at[2, 0], o_recv.at[2, 0], sib)

    def pass_rows(chunk):
        rows_at = pl.ds(chunk * chunk_rows, chunk_rows)
        return remote(
            others.at[1, rows_at], others.at[2, rows_at], o_send.at[1, chunk], o_recv.at[1, chunk], sib
        )

    def pass_on(chunk):
        arrive(lambda: side_rows(chunk))
        start(lambda: pass_rows(chunk))

    def grad_rows(slot):
        return grad_ref if slot == 0 else others.at[slot - 1]

    def exchange(s, kind, side_bit, g, src, dst, device):
        return remote(
            src, dst, s_send.at[s, kind, side_bit, g], s_recv.at[s, kind, side_bit, g], device
        )

    def pair_copy(s, b, g):
        return exchange(s, 0, b, g, pair_out.at[s, b, g], pair_in.at[s, b, g], sib)

    def chain_copy(s, b, g):
        return exchange(s, 1, b, g, chain_out.at[s, b, g], chain_in.at[s, b, g], below if s else above)

    def side_copy(s, b, g):
        return exchange(s, 2, b, g, side_out.at[s, b, g], side_in.at[s, b, g], side)

    def final_copy(s, b, g):
        return exchange(s, 3, b, g, final_out.at[s, b, g], states.at[s, c, b, g], sib)

    first = [k == 0, k == lines - 1]
    not_first = [k > 0, k < lines - 1]
    not_last = [k < lines - 1, k > 0]
    ahead = [(1 - y).astype(f32), y.astype(f32)]
    core = [c.astype(f32), (1 - c).astype(f32)]

    def pair_send(s, b, g):
        pair_out[s, b, g] = part[1 - c, b, g].astype(bf16)
        start(lambda: pair_copy(s, b, g))

    def pair_take(s, b, g):
        arrive(lambda: pair_copy(s, b, g))
        own = part[c, b, g]
        total[s, b, g] = own + pair_in[s, b, g].astype(f32)
        final_out[s, b, g] = own.astype(bf16)

    def chain_body(s, b, g, is_first):
        if is_first:
            chain_in[s, b, g] = jnp.zeros_like(chain_in[s, b, g])
        else:
            chain_copy(s, b, g).wait_recv()
        earlier = chain_in[s, b, g].astype(f32)
        mine = total[s, b, g]
        chain_out[s, b, g] = (earlier + mine).astype(bf16)
        when(not_last[s], lambda: chain_copy(s, b, g).start())
        side_out[s, b, g] = (earlier + ahead[s] * mine).astype(bf16)
        side_copy(s, b, g).start()

    def chain(s, chunks, step):
        here = (k == step) if s == 0 else (k == lines - 1 - step)

        def run():
            for b, g in chunks:
                chain_body(s, b, g, step == 0)

        when(here, run)

    def chain_pending(s, chunks):
        for b, g in chunks:
            pending.append((not_last[s], lambda b=b, g=g: chain_copy(s, b, g)))
            pending.append((True, lambda b=b, g=g: side_copy(s, b, g)))

    def finish(s, b, g):
        arrive(lambda: side_copy(s, b, g))
        base = chain_in[s, b, g].astype(f32) + side_in[s, b, g].astype(f32)
        mine = base + core[s] * pair_in[s, b, g].astype(f32)
        theirs = base + (1.0 - core[s]) * final_out[s, b, g].astype(f32)
        states[s, c, b, g] = (score_scale * mine).astype(bf16)
        final_out[s, b, g] = (score_scale * theirs).astype(bf16)
        start(lambda: final_copy(s, b, g))

    def final_take(s, b, g):
        arrive(
            lambda: exchange(s, 3, b, g, final_out.at[s, b, g], states.at[s, 1 - c, b, g], sib)
        )

    for chunk in range(CHUNKS - 1):
        start(lambda chunk=chunk: side_rows(chunk))
    start(sib_rows)
    loads[2].wait()
    for hh in range(2):
        across_send(k, 0, hh)
        line_send(False, 0, hh)

    def key_value(h):
        at = at_head(h)
        product = contract(key_ref[:, at], value_ref[:, at], 0, 0)
        return lambda: put_part(h, product)

    loads[0].wait()
    loads[1].wait()
    each(0, HEADS, 4, key_value)
    every = [(b, g) for b in range(2) for g in range(groups)]
    for b, g in every:
        pair_send(0, b, g)

    def head_scores(h):
        at = at_head(h)
        product = score_scale * contract(query_ref[:, at], key_ref[:, at], 1, 1) * causal

        def put():
            scores[h] = product.astype(bf16)

        return put

    for b, g in every:
        pair_take(0, b, g)
    chain(0, every, 0)
    for hh in range(2):
        line_send(True, 0, hh)
    loads[3].wait()
    each(0, HEADS, 4, head_scores)
    loads[4].wait()

    for hop in range(lines - 1):
        line_arrival(False, hop)
        chain(0, every, hop + 1)
        if hop == lines - 2:
            start(lambda: side_rows(CHUNKS - 1))
        line_arrival(True, hop)
        for chunk in range(CHUNKS - 1):
            if chunk * (lines - 1) // (CHUNKS - 1) == hop:
                pass_on(chunk)
    chain_pending(0, every)

    for b, g in every:
        finish(0, b, g)
    for b, g in every:
        final_take(0, b, g)

    order = [jnp.where(k == 0, groups - 1 - i, i) for i in range(groups)]

    def attend(g):
        def head_attended(h):
            at = at_head(h)
            attended = contract(scores[h], value_ref[:, at], 1, 0)
            attended = attended + contract(query_ref[:, at], state_of(0, h), 1, 0)
            turned = attended.T.astype(bf16)

            def put():
                for piece, n in enumerate(parts_of(h)):
                    member, g2, j = locate(n)
                    att_own[member, g2, pl.ds(pl.multiple_of(j * rows, rows), rows), :] = turned[
                        piece * rows : (piece + 1) * rows, :
                    ]

            return put

        each(g * (HEADS // groups), HEADS // groups, 4, head_attended)

    def att_copy(i, slot):
        g = order[i]
        return remote(
            att_own.at[members[slot], g], att_in.at[slot - 1, g],
            a_send.at[i, slot - 1], a_recv.at[i, slot - 1], peers[slot],
        )

    def head_piece(slot, g):
        rows_of = grad_rows(slot)
        product = None
        for column_block in range(data_count):
            here = pl.ds(column_block * columns, columns)
            term = contract(
                rows_of[:, here], wall[column_block, g * WIDE : (g + 1) * WIDE, :], 1, 1
            )
            product = term if product is None else product + term
        return product.astype(bf16)

    def grad_copy(slot, g):
        return remote(
            grad_send.at[slot - 1, g], head_grad.at[m, g],
            g_send.at[g, slot - 1], g_recv.at[g, slot - 1], peers[slot],
        )

    def grad_take(slot, g):
        arrive(
            lambda: remote(
                grad_send.at[slot - 1, g], head_grad.at[members[slot], g],
                g_send.at[g, slot - 1], g_recv.at[g, slot - 1], peers[slot],
            )
        )

    def send_heads(g):
        for slot in (2, 3, 1):
            grad_send[slot - 1, g] = head_piece(slot, g)
            start(functools.partial(grad_copy, slot, g))
        head_grad[m, g] = head_piece(0, g)

    for i in range(groups):
        attend(order[i])
        for slot in (2, 3, 1):
            start(functools.partial(att_copy, i, slot))
        if i == 0:
            across_arrivals()
            pass_on(CHUNKS - 1)
            arrive(sib_rows)
            for chunk in range(CHUNKS):
                arrive(lambda: pass_rows(chunk))
        send_heads(i)

    crossing = []
    for i in range(groups):
        base = order[i] * span
        for j in range(span):
            falls = (k == 0) if i == 0 else (k < lines - 1)
            crossing.append(base + jnp.where(falls, span - 1 - j, j))
    units = [jnp.where(i < k, i, lines - 1 - i + k) for i in range(lines - 1)] + [k]

    def unit_rows(t, hh):
        return pl.ds(pl.multiple_of(t * rows + hh * half, half), half)

    def weight_product(g, column_block, put):
        strip = min(columns, 512)
        for begin in range(0, columns, strip):
            here = pl.ds(pl.multiple_of(column_block * columns + begin, strip), strip)
            product = contract(att_own[m, g], grad_ref[:, here], 1, 0)
            for slot in range(1, 4):
                product = product + contract(att_in[slot - 1, g], others[slot - 1, :, here], 1, 0)
            put(slice(begin, begin + strip), grad_scale * product)

    def x_copy(u, e, t, hh):
        at = unit_rows(t, hh)
        return remote(
            x_out.at[u, e - 1, at], x_in.at[u, e - 1, at],
            xr_send.at[u, e - 1, t, hh], xr_recv.at[u, e - 1, t, hh], left if u else right,
        )

    def x_take(u, e, t, hh, condition=True):
        arrive(lambda: x_copy(u, e + 1, t, hh), condition)

    def group_rows(g):
        return pl.ds(pl.multiple_of(g * WIDE, WIDE), WIDE)

    def send_weight(i):
        g = order[i]
        for slot in (1, 2, 3):
            arrive(lambda: att_copy(i, slot))
        for e in range(data_count - 1, 0, -1):
            for u in range(2):
                valid = (d >= e) if u else (d + e < data_count)
                more = (d < data_count - 1) if u else (d > 0)
                column_block = d - e if u else d + e

                def run():
                    def put(here, value):
                        x_out[u, e - 1, group_rows(g), here] = value.astype(bf16)

                    weight_product(g, column_block, put)
                    for t in crossing[i * span : (i + 1) * span]:
                        for hh in range(2):
                            if e < data_count - 1:

                                @pl.when(more)
                                def _():
                                    x_copy(u, e + 1, t, hh).wait_recv()
                                    at = unit_rows(t, hh)
                                    x_out[u, e - 1, at] = (
                                        x_out[u, e - 1, at].astype(f32) + x_in[u, e, at].astype(f32)
                                    ).astype(bf16)

                            x_copy(u, e, t, hh).start()

                when(valid, run)
                for t in crossing[i * span : (i + 1) * span]:
                    for hh in range(2):
                        pending.append(
                            (valid, lambda u=u, e=e, t=t, hh=hh: x_copy(u, e, t, hh))
                        )

        def put_own(here, value):
            own_sum[group_rows(g), here] = value

        weight_product(g, d, put_own)

    def z_copy(u, t, hh):
        at = unit_rows(t, hh)
        return remote(
            z_out.at[at], z_in.at[u, at], zr_send.at[t, hh], zr_recv.at[u, t, hh], below if u else above
        )

    def reduce_unit(i, here=True):
        t = units[i]

        def run():
            for hh in range(2):
                at = unit_rows(t, hh)

                def add(landed):
                    own_sum[at, :] = own_sum[at, :] + landed[at, :].astype(f32)

                for u, condition in ((0, d > 0), (1, d < data_count - 1)):

                    @pl.when(condition)
                    def _():
                        x_copy(u, 1, t, hh).wait_recv()
                        add(x_in.at[u, 0])

                for u, condition in ((0, k > 0), (1, k < lines - 1)):
                    moves = True if i == lines - 1 else ((t < k) if u else (t > k))

                    @pl.when(condition & moves)
                    def _():
                        z_copy(u, t, hh).wait_recv()
                        add(z_in.at[u])

                if i == lines - 1:
                    weight_out[hh * half : (hh + 1) * half, :] = own_sum[at, :]
                    continue
                z_out[at, :] = own_sum[at, :].astype(bf16)
                for u in range(2):
                    when((t < k) if u else (t > k), lambda: z_copy(u, t, hh).start())

        when(here, run)

    def reduce_pending(i):
        t = units[i]
        for hh in range(2):
            for u in range(2):
                pending.append(
                    ((t < k) if u else (t > k), lambda u=u, t=t, hh=hh: z_copy(u, t, hh))
                )

    def query_dout(b, g):
        def body(j):
            h = head_of(b, g, j)
            product = contract(query_ref[:, at_head(h)], grad_of(h), 0, 0)
            return lambda: put_part(h, product)

        for store in [body(j) for j in range(4)]:
            store()

    def local_heads(b, g):
        def body(j):
            h = head_of(b, g, j)
            at = at_head(h)
            rows_g, rows_q, rows_k = grad_of(h), query_ref[:, at], key_ref[:, at]
            grad_scores = (
                score_scale * contract(rows_g, value_ref[:, at], 1, 1) * causal
            ).astype(bf16)
            queried = contract(grad_scores, rows_k, 1, 0) + contract(rows_g, state_of(0, h), 1, 1)
            keyed = contract(grad_scores, rows_q, 0, 0)
            valued = contract(scores[h], rows_g, 0, 0)

            def put():
                query_out[:, at] = queried.astype(bf16)
                key_sum[:, at] = keyed
                value_sum[:, at] = valued

            return put

        for store in [body(j) for j in range(4)]:
            store()

    def last_terms(b, g):
        def body(j):
            h = head_of(b, g, j)
            at = at_head(h)
            state = state_of(1, h)
            keyed = key_sum[:, at] + contract(value_ref[:, at], state, 1, 1)
            valued = value_sum[:, at] + contract(key_ref[:, at], state, 1, 0)

            def put():
                key_out[:, at] = keyed.astype(bf16)
                value_out[:, at] = valued.astype(bf16)

            return put

        for store in [body(j) for j in range(4)]:
            store()

    near = [(y, g) for g in range(groups)]
    far = [(1 - y, g) for g in range(groups)]
    lower = (k > 0) & (k < lines // 2)
    upper = (k >= lines // 2) & (k < lines - 1)

    def reduce_units(first_set, here):
        for i in range(1, span) if first_set else range(span, lines - 1):
            reduce_unit(i, here)

    def take_far(g):
        for slot in (2, 3):
            grad_take(slot, g)
        query_dout(*far[g])
        pair_send(1, *far[g])
        pair_take(1, *far[g])
        chain(1, [far[g]], 0)

    for b, g in near:
        grad_take(1, g)
        query_dout(b, g)
        pair_send(1, b, g)
    for b, g in near:
        pair_take(1, b, g)
    chain(1, near, 0)
    send_weight(0)
    for step in range(1, lines):
        if step <= groups:
            local_heads(*near[step - 1])
        chain(1, near, step)
    take_far(0)
    local_heads(*far[0])
    reduce_unit(0, (k == 0) | (k == lines - 1))
    chain(1, [far[0]], 1)
    send_weight(1)
    for step in range(2, lines):
        chain(1, [far[0]], step)
    reduce_unit(0, lower | upper)
    reduce_units(True, k == 0)
    take_far(1)
    reduce_units(True, k == lines - 1)
    local_heads(*far[1])
    chain(1, [far[1]], 1)
    reduce_units(True, lower)
    reduce_units(False, (k == 0) | (k == lines - 1))
    chain(1, [far[1]], 2)
    reduce_units(True, upper)
    for b in range(2):
        finish(1, b, 0)
    for b in range(2):
        final_take(1, b, 0)
        last_terms(b, 0)
    for step in range(3, lines):
        chain(1, [far[1]], step)
    reduce_units(False, lower | upper)
    for b in range(2):
        finish(1, b, 1)
    reduce_unit(lines - 1)
    for b in range(2):
        final_take(1, b, 1)
        last_terms(b, 1)
    chain_pending(1, near + far)
    for i in range(lines - 1):
        reduce_pending(i)

    for condition, copy in pending:
        when(condition, lambda: copy().wait_send())


def shards(queries, key_rows, value_rows, out_grad, out_weight):
    tokens, features = queries.shape[1:]
    seq_count = lax.axis_size("seq")
    data_count = lax.axis_size("dp")
    lines = seq_count // 4
    seq_length = tokens * seq_count
    score_scale = 1.0 / math.sqrt(HEAD * seq_length)
    grad_scale = 1.0 / math.sqrt(queries.shape[0] * data_count * seq_length)
    rows, columns = out_weight.shape
    width = out_grad.shape[2]
    held = lines * rows
    groups = held // WIDE
    hops = max(1, data_count - 1)
    bf16, f32 = jnp.bfloat16, jnp.float32
    vmem = pl.BlockSpec(memory_space=pltpu.VMEM)
    dma = pltpu.SemaphoreType.DMA
    flat = pltpu.VMEM((tokens, features), bf16)

    def scan(kind):
        return pltpu.VMEM((2, 2, groups, WIDE, HEAD), kind)

    query_grad, key_grad, value_grad, weight_grad = pl.pallas_call(
        functools.partial(kernel, lines, data_count, score_scale, grad_scale),
        out_shape=(flat, flat, flat, pltpu.VMEM((rows, columns), f32)),
        in_specs=[pl.BlockSpec(memory_space=pl.ANY)] * 5,
        out_specs=(vmem,) * 4,
        scratch_shapes=[
            pltpu.VMEM((tokens, features), bf16),
            pltpu.VMEM((tokens, features), bf16),
            pltpu.VMEM((tokens, features), bf16),
            pltpu.VMEM((tokens, width), bf16),
            pltpu.VMEM((data_count, held, columns), bf16),
            pltpu.VMEM((3, tokens, width), bf16),
            pltpu.VMEM((4, groups, WIDE, tokens), bf16),
            pltpu.VMEM((3, groups, WIDE, tokens), bf16),
            pltpu.VMEM((3, groups, tokens, WIDE), bf16),
            pltpu.VMEM((4, groups, tokens, WIDE), bf16),
            pltpu.VMEM((HEADS, tokens, tokens), bf16),
            pltpu.VMEM((tokens, features), f32),
            pltpu.VMEM((tokens, features), f32),
            pltpu.VMEM((2, 2, groups, WIDE, HEAD), f32),
            scan(f32),
            scan(bf16),
            scan(bf16),
            scan(bf16),
            scan(bf16),
            scan(bf16),
            scan(bf16),
            scan(bf16),
            pltpu.VMEM((2, 2, 2, groups, WIDE, HEAD), bf16),
            pltpu.VMEM((held, columns), f32),
            pltpu.VMEM((2, hops, held, columns), bf16),
            pltpu.VMEM((2, hops, held, columns), bf16),
            pltpu.VMEM((held, columns), bf16),
            pltpu.VMEM((2, held, columns), bf16),
            dma((2, lines - 1, 2)),
            dma((2, lines - 1, 2)),
            dma((2, hops, 2, lines)),
            dma((2, hops, 2, lines)),
            dma((3, CHUNKS)),
            dma((3, CHUNKS)),
            dma((groups, 3)),
            dma((groups, 3)),
            dma((groups, 3)),
            dma((groups, 3)),
            dma((2, 4, 2, groups)),
            dma((2, 4, 2, groups)),
            dma((2, hops, lines, 2)),
            dma((2, hops, lines, 2)),
            dma((lines, 2)),
            dma((2, lines, 2)),
            dma((5,)),
        ],
        compiler_params=pltpu.CompilerParams(
            collective_id=0, has_side_effects=True, vmem_limit_bytes=58 << 20
        ),
    )(queries[0], key_rows[0], value_rows[0], out_grad[0], out_weight)
    return query_grad[None], key_grad[None], value_grad[None], weight_grad


def solution(mesh):
    return jax.shard_map(
        shards,
        mesh=mesh,
        in_specs=(
            P("dp", "seq", None),
            P("dp", "seq", None),
            P("dp", "seq", None),
            P("dp", "seq", None),
            P("seq", "dp"),
        ),
        out_specs=(
            P("dp", "seq", None),
            P("dp", "seq", None),
            P("dp", "seq", None),
            P("seq", "dp"),
        ),
        check_vma=False,
    )
```

```python
import functools
import math

import jax
import jax.numpy as jnp
from jax import lax
from jax.experimental import pallas as pl
from jax.experimental.pallas import tpu as pltpu
from jax.sharding import PartitionSpec as P

HEADS = 16
HEAD = 128
WIDE = 256
CHUNKS = 4
MESH = pl.DeviceIdType.MESH


def remote(src, dst, send, recv, device):
    return pltpu.make_async_remote_copy(
        src_ref=src, dst_ref=dst, send_sem=send, recv_sem=recv, device_id=device, device_id_type=MESH
    )


def contract(left, right, left_dim, right_dim):
    return lax.dot_general(
        left, right, (((left_dim,), (right_dim,)), ((), ())), preferred_element_type=jnp.float32
    )


def each(begin, count, together, body):
    @pl.loop(0, count, step=together)
    def _(j):
        for store in [body(begin + j + i) for i in range(together)]:
            store()


def kernel(
    lines, data_count, score_scale, grad_scale,
    query_hbm, key_hbm, value_hbm, grad_hbm, weight_hbm,
    query_out, key_out, value_out, weight_out,
    query_ref, key_ref, value_ref, grad_ref, wall, others, att_own, att_in, grad_send, head_grad, scores, key_sum, value_sum,
    part, total, pair_out, pair_in, chain_in, chain_out, side_in, side_out, final_out, states,
    own_sum, x_out, x_in, z_out, z_in,
    zg_send, zg_recv, xg_send, xg_recv, o_send, o_recv, a_send, a_recv, g_send, g_recv,
    s_send, s_recv, xr_send, xr_recv, zr_send, zr_recv, load_sem,
):
    f32, bf16 = jnp.float32, jnp.bfloat16
    seq, d = lax.axis_index("seq"), lax.axis_index("dp")
    k, m, y, c = seq // 4, seq % 4, (seq // 2) % 2, seq % 2
    rows, columns = weight_hbm.shape
    half = rows // 2
    tokens = grad_ref.shape[0]
    span = WIDE // rows
    groups = lines // span
    per_pair = 2 * rows // HEAD
    pieces = HEAD // rows
    members = [m, m + 1 - 2 * c, m + 2 - 4 * y, 3 - m]
    peers = [{"seq": seq - m + member} for member in members]
    sib, side = peers[1], peers[2]
    above, below = {"seq": seq + 4}, {"seq": seq - 4}
    right, left = {"dp": d + 1}, {"dp": d - 1}
    causal = (
        lax.broadcasted_iota(jnp.int32, (tokens, tokens), 0)
        >= lax.broadcasted_iota(jnp.int32, (tokens, tokens), 1)
    ).astype(f32)
    pending = []

    def when(condition, body):
        if condition is True:
            body()
        elif condition is not False:
            pl.when(condition)(body)

    def start(copy, condition=True):
        when(condition, lambda: copy().start())
        pending.append((condition, copy))

    def arrive(copy, condition=True):
        when(condition, lambda: copy().wait_recv())

    own_rows = wall.at[d, pl.ds(pl.multiple_of(k * rows, rows), rows)]
    loads = [
        pltpu.make_async_copy(src, dst, load_sem.at[i])
        for i, (src, dst) in enumerate(
            (
                (key_hbm, key_ref), (value_hbm, value_ref), (weight_hbm, own_rows),
                (query_hbm, query_ref), (grad_hbm, grad_ref),
            )
        )
    ]
    for load in loads:
        load.start()
    barrier = pltpu.get_barrier_semaphore()
    neighbours = [(True, peer) for peer in peers[1:]]
    neighbours += [(k < lines - 1, above), (k > 0, below), (d < data_count - 1, right), (d > 0, left)]
    for condition, device in neighbours:
        when(
            condition,
            lambda device=device: pl.semaphore_signal(
                barrier, inc=1, device_id=device, device_id_type=MESH
            ),
        )
    pl.semaphore_wait(
        barrier,
        sum(1 if condition is True else jnp.where(condition, 1, 0) for condition, _ in neighbours),
    )

    def at_head(h):
        return pl.ds(pl.multiple_of(h * HEAD, HEAD), HEAD)

    def parts_of(h):
        return [h * pieces + piece for piece in range(pieces)]

    def locate(n):
        line = n // 4
        return n % 4, line // span, line % span

    def state_of(index, h):
        found = []
        for n in parts_of(h):
            member, g, j = locate(n)
            found.append(
                states[index, member % 2, member // 2, g, pl.ds(pl.multiple_of(j * rows, rows), rows), :]
            )
        return found[0] if pieces == 1 else jnp.concatenate(found, axis=0)

    def put_part(h, product):
        for piece, n in enumerate(parts_of(h)):
            member, g, j = locate(n)
            part[member % 2, member // 2, g, pl.ds(pl.multiple_of(j * rows, rows), rows), :] = product[
                piece * rows : (piece + 1) * rows, :
            ]

    def grad_of(h):
        found = []
        for n in parts_of(h):
            member, g, j = locate(n)
            if pieces == 1:
                return head_grad[member, g, :, pl.ds(pl.multiple_of(j * rows, rows), rows)]
            lane = pl.ds(pl.multiple_of(j // pieces * HEAD, HEAD), HEAD)
            block = head_grad[member, g, :, lane]
            piece = block[:, :rows]
            for i in range(1, pieces):
                piece = jnp.where(j % pieces == i, block[:, i * rows : (i + 1) * rows], piece)
            found.append(piece)
        return jnp.concatenate(found, axis=1)

    def head_of(side_bit, g, j):
        return (2 * (g * span + j // per_pair) + side_bit) * per_pair + j % per_pair

    def block_of(line, hh, column_block):
        return wall.at[column_block, pl.ds(pl.multiple_of(line * rows + hh * half, half), half)]

    def line_hop(up, hop, hh):
        line = k - hop if up else k + hop
        block = block_of(line, hh, d)
        u = int(up)
        return remote(block, block, zg_send.at[u, hop, hh], zg_recv.at[u, hop, hh], above if up else below)

    def line_send(up, hop, hh):
        valid = ((k >= hop) & (k < lines - 1)) if up else ((k + hop < lines) & (k > 0))
        start(lambda: line_hop(up, hop, hh), valid)

    def across(line, hop, hh, to_right):
        block = block_of(line, hh, d - hop if to_right else d + hop)
        u = int(to_right)
        return remote(
            block, block, xg_send.at[u, hop, hh, line], xg_recv.at[u, hop, hh, line],
            right if to_right else left,
        )

    def across_send(line, hop, hh, condition=True):
        for to_right in (True, False):
            if to_right:
                valid = (d >= hop) & (d < data_count - 1) & condition
            else:
                valid = (d + hop < data_count) & (d > 0) & condition
            start(lambda to_right=to_right: across(line, hop, hh, to_right), valid)

    def line_arrival(up, hop):
        line = k - 1 - hop if up else k + 1 + hop
        valid = (line >= 0) if up else (line < lines)
        for hh in range(2):
            block = block_of(line, hh, d)
            u = int(up)
            arrive(
                lambda: remote(block, block, zg_send.at[u, hop, hh], zg_recv.at[u, hop, hh], sib), valid
            )
            if hop + 1 < lines - 1:
                line_send(up, hop + 1, hh)
            across_send(line, 0, hh, valid)

    def across_arrivals():
        for hop in range(data_count - 1):
            for line in range(lines):
                for hh in range(2):
                    for to_right in (True, False):
                        u = int(to_right)
                        owner = d - 1 - hop if to_right else d + 1 + hop
                        valid = (owner >= 0) if to_right else (owner < data_count)
                        arrive(
                            lambda: remote(
                                block_of(line, hh, owner), block_of(line, hh, owner),
                                xg_send.at[u, hop, hh, line], xg_recv.at[u, hop, hh, line], sib,
                            ),
                            valid,
                        )
                    if hop + 1 < data_count - 1:
                        across_send(line, hop + 1, hh)

    chunk_rows = tokens // CHUNKS

    def side_rows(chunk):
        rows_at = pl.ds(chunk * chunk_rows, chunk_rows)
        return remote(
            grad_hbm.at[rows_at], others.at[1, rows_at], o_send.at[0, chunk], o_recv.at[0, chunk], side
        )

    def sib_rows():
        return remote(grad_hbm, others.at[0], o_send.at[2, 0], o_recv.at[2, 0], sib)

    def pass_rows(chunk):
        rows_at = pl.ds(chunk * chunk_rows, chunk_rows)
        return remote(
            others.at[1, rows_at], others.at[2, rows_at], o_send.at[1, chunk], o_recv.at[1, chunk], sib
        )

    def pass_on(chunk):
        arrive(lambda: side_rows(chunk))
        start(lambda: pass_rows(chunk))

    def grad_rows(slot):
        return grad_ref if slot == 0 else others.at[slot - 1]

    def exchange(s, kind, side_bit, g, src, dst, device):
        return remote(
            src, dst, s_send.at[s, kind, side_bit, g], s_recv.at[s, kind, side_bit, g], device
        )

    def pair_copy(s, b, g):
        return exchange(s, 0, b, g, pair_out.at[s, b, g], pair_in.at[s, b, g], sib)

    def chain_copy(s, b, g):
        return exchange(s, 1, b, g, chain_out.at[s, b, g], chain_in.at[s, b, g], below if s else above)

    def side_copy(s, b, g):
        return exchange(s, 2, b, g, side_out.at[s, b, g], side_in.at[s, b, g], side)

    def final_copy(s, b, g):
        return exchange(s, 3, b, g, final_out.at[s, b, g], states.at[s, c, b, g], sib)

    first = [k == 0, k == lines - 1]
    not_first = [k > 0, k < lines - 1]
    not_last = [k < lines - 1, k > 0]
    ahead = [(1 - y).astype(f32), y.astype(f32)]
    core = [c.astype(f32), (1 - c).astype(f32)]

    def pair_send(s, b, g):
        pair_out[s, b, g] = part[1 - c, b, g].astype(bf16)
        start(lambda: pair_copy(s, b, g))

    def pair_take(s, b, g):
        arrive(lambda: pair_copy(s, b, g))
        own = part[c, b, g]
        total[s, b, g] = own + pair_in[s, b, g].astype(f32)
        final_out[s, b, g] = own.astype(bf16)

    def chain_body(s, b, g, is_first):
        if is_first:
            chain_in[s, b, g] = jnp.zeros_like(chain_in[s, b, g])
        else:
            chain_copy(s, b, g).wait_recv()
        earlier = chain_in[s, b, g].astype(f32)
        mine = total[s, b, g]
        chain_out[s, b, g] = (earlier + mine).astype(bf16)
        when(not_last[s], lambda: chain_copy(s, b, g).start())
        side_out[s, b, g] = (earlier + ahead[s] * mine).astype(bf16)
        side_copy(s, b, g).start()

    def chain(s, chunks, step):
        here = (k == step) if s == 0 else (k == lines - 1 - step)

        def run():
            for b, g in chunks:
                chain_body(s, b, g, step == 0)

        when(here, run)

    def chain_pending(s, chunks):
        for b, g in chunks:
            pending.append((not_last[s], lambda b=b, g=g: chain_copy(s, b, g)))
            pending.append((True, lambda b=b, g=g: side_copy(s, b, g)))

    def finish(s, b, g):
        arrive(lambda: side_copy(s, b, g))
        base = chain_in[s, b, g].astype(f32) + side_in[s, b, g].astype(f32)
        mine = base + core[s] * pair_in[s, b, g].astype(f32)
        theirs = base + (1.0 - core[s]) * final_out[s, b, g].astype(f32)
        states[s, c, b, g] = (score_scale * mine).astype(bf16)
        final_out[s, b, g] = (score_scale * theirs).astype(bf16)
        start(lambda: final_copy(s, b, g))

    def final_take(s, b, g):
        arrive(
            lambda: exchange(s, 3, b, g, final_out.at[s, b, g], states.at[s, 1 - c, b, g], sib)
        )

    for chunk in range(CHUNKS - 1):
        start(lambda chunk=chunk: side_rows(chunk))
    start(sib_rows)
    loads[2].wait()
    for hh in range(2):
        across_send(k, 0, hh)
        line_send(False, 0, hh)

    def key_value(h):
        at = at_head(h)
        product = contract(key_ref[:, at], value_ref[:, at], 0, 0)
        return lambda: put_part(h, product)

    loads[0].wait()
    loads[1].wait()
    each(0, HEADS, 4, key_value)
    every = [(b, g) for b in range(2) for g in range(groups)]
    for b, g in every:
        pair_send(0, b, g)

    def head_scores(h):
        at = at_head(h)
        product = score_scale * contract(query_ref[:, at], key_ref[:, at], 1, 1) * causal

        def put():
            scores[h] = product.astype(bf16)

        return put

    for b, g in every:
        pair_take(0, b, g)
    chain(0, every, 0)
    for hh in range(2):
        line_send(True, 0, hh)
    loads[3].wait()
    each(0, HEADS, 4, head_scores)
    loads[4].wait()

    for hop in range(lines - 1):
        line_arrival(False, hop)
        chain(0, every, hop + 1)
        if hop == lines - 2:
            start(lambda: side_rows(CHUNKS - 1))
        line_arrival(True, hop)
        for chunk in range(CHUNKS - 1):
            if chunk * (lines - 1) // (CHUNKS - 1) == hop:
                pass_on(chunk)
    chain_pending(0, every)

    for b, g in every:
        finish(0, b, g)
    for b, g in every:
        final_take(0, b, g)

    order = [jnp.where(k == 0, groups - 1 - i, i) for i in range(groups)]

    def attend(g):
        def head_attended(h):
            at = at_head(h)
            attended = contract(scores[h], value_ref[:, at], 1, 0)
            attended = attended + contract(query_ref[:, at], state_of(0, h), 1, 0)
            turned = attended.T.astype(bf16)

            def put():
                for piece, n in enumerate(parts_of(h)):
                    member, g2, j = locate(n)
                    att_own[member, g2, pl.ds(pl.multiple_of(j * rows, rows), rows), :] = turned[
                        piece * rows : (piece + 1) * rows, :
                    ]

            return put

        each(g * (HEADS // groups), HEADS // groups, 4, head_attended)

    def att_copy(i, slot):
        g = order[i]
        return remote(
            att_own.at[members[slot], g], att_in.at[slot - 1, g],
            a_send.at[i, slot - 1], a_recv.at[i, slot - 1], peers[slot],
        )

    def head_piece(slot, g):
        rows_of = grad_rows(slot)
        product = None
        for column_block in range(data_count):
            here = pl.ds(column_block * columns, columns)
            term = contract(
                rows_of[:, here], wall[column_block, g * WIDE : (g + 1) * WIDE, :], 1, 1
            )
            product = term if product is None else product + term
        return product.astype(bf16)

    def grad_copy(slot, g):
        return remote(
            grad_send.at[slot - 1, g], head_grad.at[m, g],
            g_send.at[g, slot - 1], g_recv.at[g, slot - 1], peers[slot],
        )

    def grad_take(slot, g):
        arrive(
            lambda: remote(
                grad_send.at[slot - 1, g], head_grad.at[members[slot], g],
                g_send.at[g, slot - 1], g_recv.at[g, slot - 1], peers[slot],
            )
        )

    def send_heads(g):
        for slot in (2, 3, 1):
            grad_send[slot - 1, g] = head_piece(slot, g)
            start(functools.partial(grad_copy, slot, g))
        head_grad[m, g] = head_piece(0, g)

    for i in range(groups):
        attend(order[i])
        for slot in (2, 3, 1):
            start(functools.partial(att_copy, i, slot))
        if i == 0:
            across_arrivals()
            pass_on(CHUNKS - 1)
            arrive(sib_rows)
            for chunk in range(CHUNKS):
                arrive(lambda: pass_rows(chunk))
        send_heads(i)

    crossing = []
    for i in range(groups):
        base = order[i] * span
        for j in range(span):
            falls = (k == 0) if i == 0 else (k < lines - 1)
            crossing.append(base + jnp.where(falls, span - 1 - j, j))
    units = [jnp.where(i < k, i, lines - 1 - i + k) for i in range(lines - 1)] + [k]

    def unit_rows(t, hh):
        return pl.ds(pl.multiple_of(t * rows + hh * half, half), half)

    def weight_product(g, column_block, put):
        strip = min(columns, 512)
        for begin in range(0, columns, strip):
            here = pl.ds(pl.multiple_of(column_block * columns + begin, strip), strip)
            product = contract(att_own[m, g], grad_ref[:, here], 1, 0)
            for slot in range(1, 4):
                product = product + contract(att_in[slot - 1, g], others[slot - 1, :, here], 1, 0)
            put(slice(begin, begin + strip), grad_scale * product)

    def x_copy(u, e, t, hh):
        at = unit_rows(t, hh)
        return remote(
            x_out.at[u, e - 1, at], x_in.at[u, e - 1, at],
            xr_send.at[u, e - 1, t, hh], xr_recv.at[u, e - 1, t, hh], left if u else right,
        )

    def x_take(u, e, t, hh, condition=True):
        arrive(lambda: x_copy(u, e + 1, t, hh), condition)

    def group_rows(g):
        return pl.ds(pl.multiple_of(g * WIDE, WIDE), WIDE)

    def send_weight(i):
        g = order[i]
        for slot in (1, 2, 3):
            arrive(lambda: att_copy(i, slot))
        for e in range(data_count - 1, 0, -1):
            for u in range(2):
                valid = (d >= e) if u else (d + e < data_count)
                more = (d < data_count - 1) if u else (d > 0)
                column_block = d - e if u else d + e

                def run():
                    def put(here, value):
                        x_out[u, e - 1, group_rows(g), here] = value.astype(bf16)

                    weight_product(g, column_block, put)
                    for t in crossing[i * span : (i + 1) * span]:
                        for hh in range(2):
                            if e < data_count - 1:

                                @pl.when(more)
                                def _():
                                    x_copy(u, e + 1, t, hh).wait_recv()
                                    at = unit_rows(t, hh)
                                    x_out[u, e - 1, at] = (
                                        x_out[u, e - 1, at].astype(f32) + x_in[u, e, at].astype(f32)
                                    ).astype(bf16)

                            x_copy(u, e, t, hh).start()

                when(valid, run)
                for t in crossing[i * span : (i + 1) * span]:
                    for hh in range(2):
                        pending.append(
                            (valid, lambda u=u, e=e, t=t, hh=hh: x_copy(u, e, t, hh))
                        )

        def put_own(here, value):
            own_sum[group_rows(g), here] = value

        weight_product(g, d, put_own)

    def z_copy(u, t, hh):
        at = unit_rows(t, hh)
        return remote(
            z_out.at[at], z_in.at[u, at], zr_send.at[t, hh], zr_recv.at[u, t, hh], below if u else above
        )

    def reduce_unit(i, here=True):
        t = units[i]

        def run():
            for hh in range(2):
                at = unit_rows(t, hh)

                def add(landed):
                    own_sum[at, :] = own_sum[at, :] + landed[at, :].astype(f32)

                for u, condition in ((0, d > 0), (1, d < data_count - 1)):

                    @pl.when(condition)
                    def _():
                        x_copy(u, 1, t, hh).wait_recv()
                        add(x_in.at[u, 0])

                for u, condition in ((0, k > 0), (1, k < lines - 1)):
                    moves = True if i == lines - 1 else ((t < k) if u else (t > k))

                    @pl.when(condition & moves)
                    def _():
                        z_copy(u, t, hh).wait_recv()
                        add(z_in.at[u])

                if i == lines - 1:
                    weight_out[hh * half : (hh + 1) * half, :] = own_sum[at, :]
                    continue
                z_out[at, :] = own_sum[at, :].astype(bf16)
                for u in range(2):
                    when((t < k) if u else (t > k), lambda: z_copy(u, t, hh).start())

        when(here, run)

    def reduce_pending(i):
        t = units[i]
        for hh in range(2):
            for u in range(2):
                pending.append(
                    ((t < k) if u else (t > k), lambda u=u, t=t, hh=hh: z_copy(u, t, hh))
                )

    def query_dout(b, g):
        def body(j):
            h = head_of(b, g, j)
            product = contract(query_ref[:, at_head(h)], grad_of(h), 0, 0)
            return lambda: put_part(h, product)

        for store in [body(j) for j in range(4)]:
            store()

    def local_heads(b, g):
        def body(j):
            h = head_of(b, g, j)
            at = at_head(h)
            rows_g, rows_q, rows_k = grad_of(h), query_ref[:, at], key_ref[:, at]
            grad_scores = (
                score_scale * contract(rows_g, value_ref[:, at], 1, 1) * causal
            ).astype(bf16)
            queried = contract(grad_scores, rows_k, 1, 0) + contract(rows_g, state_of(0, h), 1, 1)
            keyed = contract(grad_scores, rows_q, 0, 0)
            valued = contract(scores[h], rows_g, 0, 0)

            def put():
                query_out[:, at] = queried.astype(bf16)
                key_sum[:, at] = keyed
                value_sum[:, at] = valued

            return put

        for store in [body(j) for j in range(4)]:
            store()

    def last_terms(b, g):
        def body(j):
            h = head_of(b, g, j)
            at = at_head(h)
            state = state_of(1, h)
            keyed = key_sum[:, at] + contract(value_ref[:, at], state, 1, 1)
            valued = value_sum[:, at] + contract(key_ref[:, at], state, 1, 0)

            def put():
                key_out[:, at] = keyed.astype(bf16)
                value_out[:, at] = valued.astype(bf16)

            return put

        for store in [body(j) for j in range(4)]:
            store()

    near = [(y, g) for g in range(groups)]
    far = [(1 - y, g) for g in range(groups)]
    lower = (k > 0) & (k < lines // 2)
    upper = (k >= lines // 2) & (k < lines - 1)

    def reduce_units(first_set, here):
        for i in range(1, span) if first_set else range(span, lines - 1):
            reduce_unit(i, here)

    def take_far(g):
        for slot in (2, 3):
            grad_take(slot, g)
        query_dout(*far[g])
        pair_send(1, *far[g])
        pair_take(1, *far[g])
        chain(1, [far[g]], 0)

    for b, g in near:
        grad_take(1, g)
        query_dout(b, g)
        pair_send(1, b, g)
    for b, g in near:
        pair_take(1, b, g)
    chain(1, near, 0)
    send_weight(0)
    for step in range(1, lines):
        if step <= groups:
            local_heads(*near[step - 1])
        chain(1, near, step)
    take_far(0)
    local_heads(*far[0])
    reduce_unit(0, (k == 0) | (k == lines - 1))
    chain(1, [far[0]], 1)
    send_weight(1)
    for step in range(2, lines):
        chain(1, [far[0]], step)
    reduce_units(True, k == 0)
    take_far(1)
    reduce_unit(0, lower | upper)
    reduce_units(True, k == lines - 1)
    local_heads(*far[1])
    chain(1, [far[1]], 1)
    reduce_units(True, lower)
    reduce_units(False, (k == 0) | (k == lines - 1))
    chain(1, [far[1]], 2)
    reduce_units(True, upper)
    for b in range(2):
        finish(1, b, 0)
    for b in range(2):
        final_take(1, b, 0)
        last_terms(b, 0)
    for step in range(3, lines):
        chain(1, [far[1]], step)
    reduce_units(False, lower | upper)
    for b in range(2):
        finish(1, b, 1)
    reduce_unit(lines - 1)
    for b in range(2):
        final_take(1, b, 1)
        last_terms(b, 1)
    chain_pending(1, near + far)
    for i in range(lines - 1):
        reduce_pending(i)

    for condition, copy in pending:
        when(condition, lambda: copy().wait_send())


def shards(queries, key_rows, value_rows, out_grad, out_weight):
    tokens, features = queries.shape[1:]
    seq_count = lax.axis_size("seq")
    data_count = lax.axis_size("dp")
    lines = seq_count // 4
    seq_length = tokens * seq_count
    score_scale = 1.0 / math.sqrt(HEAD * seq_length)
    grad_scale = 1.0 / math.sqrt(queries.shape[0] * data_count * seq_length)
    rows, columns = out_weight.shape
    width = out_grad.shape[2]
    held = lines * rows
    groups = held // WIDE
    hops = max(1, data_count - 1)
    bf16, f32 = jnp.bfloat16, jnp.float32
    vmem = pl.BlockSpec(memory_space=pltpu.VMEM)
    dma = pltpu.SemaphoreType.DMA
    flat = pltpu.VMEM((tokens, features), bf16)

    def scan(kind):
        return pltpu.VMEM((2, 2, groups, WIDE, HEAD), kind)

    query_grad, key_grad, value_grad, weight_grad = pl.pallas_call(
        functools.partial(kernel, lines, data_count, score_scale, grad_scale),
        out_shape=(flat, flat, flat, pltpu.VMEM((rows, columns), f32)),
        in_specs=[pl.BlockSpec(memory_space=pl.ANY)] * 5,
        out_specs=(vmem,) * 4,
        scratch_shapes=[
            pltpu.VMEM((tokens, features), bf16),
            pltpu.VMEM((tokens, features), bf16),
            pltpu.VMEM((tokens, features), bf16),
            pltpu.VMEM((tokens, width), bf16),
            pltpu.VMEM((data_count, held, columns), bf16),
            pltpu.VMEM((3, tokens, width), bf16),
            pltpu.VMEM((4, groups, WIDE, tokens), bf16),
            pltpu.VMEM((3, groups, WIDE, tokens), bf16),
            pltpu.VMEM((3, groups, tokens, WIDE), bf16),
            pltpu.VMEM((4, groups, tokens, WIDE), bf16),
            pltpu.VMEM((HEADS, tokens, tokens), bf16),
            pltpu.VMEM((tokens, features), f32),
            pltpu.VMEM((tokens, features), f32),
            pltpu.VMEM((2, 2, groups, WIDE, HEAD), f32),
            scan(f32),
            scan(bf16),
            scan(bf16),
            scan(bf16),
            scan(bf16),
            scan(bf16),
            scan(bf16),
            scan(bf16),
            pltpu.VMEM((2, 2, 2, groups, WIDE, HEAD), bf16),
            pltpu.VMEM((held, columns), f32),
            pltpu.VMEM((2, hops, held, columns), bf16),
            pltpu.VMEM((2, hops, held, columns), bf16),
            pltpu.VMEM((held, columns), bf16),
            pltpu.VMEM((2, held, columns), bf16),
            dma((2, lines - 1, 2)),
            dma((2, lines - 1, 2)),
            dma((2, hops, 2, lines)),
            dma((2, hops, 2, lines)),
            dma((3, CHUNKS)),
            dma((3, CHUNKS)),
            dma((groups, 3)),
            dma((groups, 3)),
            dma((groups, 3)),
            dma((groups, 3)),
            dma((2, 4, 2, groups)),
            dma((2, 4, 2, groups)),
            dma((2, hops, lines, 2)),
            dma((2, hops, lines, 2)),
            dma((lines, 2)),
            dma((2, lines, 2)),
            dma((5,)),
        ],
        compiler_params=pltpu.CompilerParams(
            collective_id=0, has_side_effects=True, vmem_limit_bytes=58 << 20
        ),
    )(queries[0], key_rows[0], value_rows[0], out_grad[0], out_weight)
    return query_grad[None], key_grad[None], value_grad[None], weight_grad


def solution(mesh):
    return jax.shard_map(
        shards,
        mesh=mesh,
        in_specs=(
            P("dp", "seq", None),
            P("dp", "seq", None),
            P("dp", "seq", None),
            P("dp", "seq", None),
            P("seq", "dp"),
        ),
        out_specs=(
            P("dp", "seq", None),
            P("dp", "seq", None),
            P("dp", "seq", None),
            P("seq", "dp"),
        ),
        check_vma=False,
    )
```
